32 devices in a mesh: node: 8 (over z, core), edge: 4 (over y, x).
Axes of the slice: x: 2, y: 2, z: 4, core: 2. Of those that a mesh axis runs over, the one named last changes fastest.
Arguments:
- node_feats: bfloat16 [4096, 512], P(('node', 'edge')), may hold values from -40 to 40
- members: int32 [8, 4, 3072], P('node', None, 'edge'), may hold values from 0 to 511, as said below
- incidence_mask: int32 [8, 4, 3072], P('node', None, 'edge'), may hold values from 0 to 1
- degrees: int32 [3072], P(('edge', 'node')), may hold values from 0 to 32, as said below
- w_query: bfloat16 [512, 512], replicated, may hold values from -1 to 1
- w_key: bfloat16 [512, 512], replicated, may hold values from -1 to 1
- w_value: bfloat16 [512, 512], replicated, may hold values from -0.25 to 0.25
- w_out: bfloat16 [512, 512], replicated, may hold values from -0.5 to 0.5
Outputs:
- mixed: bfloat16 [3072, 512], P(('edge', 'node'))
The draws below stay inside these ranges and needn't reach their ends.
Inputs may be any that keep to these rules, and one draw needn't show every extreme that they name: `members`: node index within the partition; only slots whose incidence_mask is 1 count. degrees[h] is the number of slots of hyperedge h over all partitions whose incidence_mask is 1; some hyperedge has every slot of every partition filled, and some hyperedge has none.
All inputs are finite; a program needn't handle non-finite values.
Results may differ from the reference program's by a relative error of at most 0.012.
Values may be sent and summed in bfloat16 or wider, within the bound.
No kernel may reach another device: no remote copies, remote signals or barrier semaphores. Data moves between devices by JAX's collectives and lax.ppermute only.
A program may use at most 64 MiB of HBM per device.

```python
import jax
import jax.numpy as jnp
from jax import lax

D = 512
SLOTS = 4
NODE_DEV = 128
NODE_PART = 512
PARTITIONS = 8
EDGE_DEV = 768
EDGES = 3072
NODES = 4096


def incidence_tables(key):
    base = jax.random.fold_in(key, 7)
    key_members = jax.random.fold_in(base, 1)
    key_level = jax.random.fold_in(base, 2)
    key_active = jax.random.fold_in(base, 3)
    key_alive = jax.random.fold_in(base, 4)
    key_slots = jax.random.fold_in(base, 5)
    key_full = jax.random.fold_in(base, 6)
    key_home = jax.random.fold_in(base, 8)
    key_coin = jax.random.fold_in(base, 9)
    key_near = jax.random.fold_in(base, 10)
    shard_count = EDGES // EDGE_DEV
    block_count = NODE_PART // NODE_DEV
    spread_table = jax.random.randint(key_members, (PARTITIONS, SLOTS, EDGES), 0, NODE_PART, dtype=jnp.int32)
    home_order = (jax.random.permutation(key_home, shard_count).astype(jnp.int32) % block_count).astype(jnp.int32)
    shard_of = jnp.arange(EDGES, dtype=jnp.int32) // EDGE_DEV
    home = jnp.take(home_order, shard_of, axis=0).astype(jnp.int32)
    coin = jax.random.randint(key_coin, (PARTITIONS, SLOTS, EDGES), 0, 2, dtype=jnp.int32) == 0
    near = jax.random.randint(key_near, (PARTITIONS, SLOTS, EDGES), 0, NODE_DEV, dtype=jnp.int32)
    member_table = jnp.where(coin, home[None, None, :] * NODE_DEV + near, spread_table).astype(jnp.int32)
    level = jax.random.randint(key_level, (PARTITIONS, 1, 1), 4, 33, dtype=jnp.int32)
    active = jax.random.randint(key_active, (PARTITIONS, 1, EDGES // 64), 0, 4, dtype=jnp.int32) != 0
    active = jnp.repeat(active, 64, axis=2)
    alive = jax.random.randint(key_alive, (1, 1, EDGES), 0, 16, dtype=jnp.int32) != 0
    chosen = jax.random.randint(key_slots, (PARTITIONS, SLOTS, EDGES), 0, 64, dtype=jnp.int32) < level
    valid = jnp.where(chosen & active & alive, 1, 0).astype(jnp.int32)
    full_edge = jax.random.randint(key_full, (), 0, EDGES, dtype=jnp.int32)
    empty_edge = (full_edge + EDGES // 2) % EDGES
    positions = jnp.arange(EDGES, dtype=jnp.int32)[None, None, :]
    valid = jnp.where(positions == full_edge, 1, valid)
    valid = jnp.where(positions == empty_edge, 0, valid).astype(jnp.int32)
    counts = jnp.sum(valid, axis=(0, 1)).astype(jnp.int32)
    return (member_table, valid, counts)


def draw_members(key, part):
    return incidence_tables(key)[0]


def draw_incidence_mask(key, part):
    return incidence_tables(key)[1]


def draw_degrees(key, part):
    return incidence_tables(key)[2]


def draw_node_feats(key, part):
    key_mean = jax.random.fold_in(key, 11)
    key_cols = jax.random.fold_in(key, 12)
    key_rows = jax.random.fold_in(key, 13)
    key_noise = jax.random.fold_in(key, 14)
    key_offset = jax.random.fold_in(key, 15)
    block_count = NODE_PART // NODE_DEV
    block_of = jnp.arange(NODES, dtype=jnp.int32) % NODE_PART // NODE_DEV
    common = jax.random.truncated_normal(key_mean, -4.0, 4.0, (1, D), jnp.float32)
    col_scale = jnp.exp(jax.random.uniform(key_cols, (1, D), jnp.float32, jnp.log(0.5), jnp.log(2.0)))
    offset_table = jax.random.truncated_normal(key_offset, -4.0, 4.0, (block_count, D), jnp.float32)
    row_offset = jnp.take(offset_table, block_of, axis=0)
    row_scale = jnp.exp(jax.random.uniform(key_rows, (NODES, 1), jnp.float32, jnp.log(0.3), jnp.log(3.0)))
    noise = jax.random.truncated_normal(key_noise, -4.0, 4.0, (NODES, D), jnp.float32)
    values = 0.1 * common + 0.6 * row_offset + row_scale * col_scale * noise
    return values.astype(jnp.bfloat16)


def gaussian(stream_key, dims, deviation, limit, kind=jnp.bfloat16):
    entries = jax.random.normal(stream_key, dims, jnp.float32) * deviation
    return jnp.minimum(jnp.maximum(entries, -limit), limit).astype(kind)


def setup_inputs(seed: int = 0) -> dict:
    keys = jax.random.split(jax.random.key(seed), 9)
    node_feats = draw_node_feats(jax.random.fold_in(keys[8], 71), 0)
    members = draw_members(jax.random.fold_in(keys[8], 71), 0)
    incidence_mask = draw_incidence_mask(jax.random.fold_in(keys[8], 71), 0)
    degrees = draw_degrees(jax.random.fold_in(keys[8], 71), 0)
    w_query = gaussian(keys[4], (D, D), (D // 16) ** -0.5, 1.0)
    w_key = gaussian(keys[5], (D, D), (D // 16) ** -0.5, 1.0)
    w_value = gaussian(keys[6], (D, D), D ** -0.5, 0.25)
    w_out = gaussian(keys[7], (D, D), (D // 4) ** -0.5, 0.5)
    return dict(node_feats=node_feats, members=members, incidence_mask=incidence_mask, degrees=degrees, w_query=w_query, w_key=w_key, w_value=w_value, w_out=w_out)


def feature_map(values):
    return jax.nn.elu(values) + 1.0


def reference(node_feats, members, incidence_mask, degrees, w_query, w_key, w_value, w_out):
    def add_partition(total, part_index):
        first_row = (part_index * NODE_PART).astype(jnp.int32)
        part_rows = lax.dynamic_slice_in_dim(node_feats, first_row, NODE_PART, 0)
        part_members = lax.dynamic_index_in_dim(members, part_index, 0, keepdims=False)
        part_valid = lax.dynamic_index_in_dim(incidence_mask, part_index, 0, keepdims=False)
        partial_value = jnp.zeros((EDGES, D), jnp.float32)
        for slot in range(SLOTS):
            picked = jnp.take(part_rows, part_members[slot], axis=0).astype(jnp.float32)
            partial_value = partial_value + picked * part_valid[slot][:, None].astype(jnp.float32)
        rounded = lax.optimization_barrier(partial_value.astype(jnp.bfloat16))
        return total + rounded.astype(jnp.float32), None

    hedge_sum, _ = lax.scan(add_partition, jnp.zeros((EDGES, D), jnp.float32), jnp.arange(PARTITIONS, dtype=jnp.int32))
    scale = jnp.maximum(degrees, 1).astype(jnp.float32)
    hedge = (hedge_sum / scale[:, None]).astype(jnp.bfloat16)
    query_proj = jnp.dot(hedge, w_query, preferred_element_type=jnp.float32)
    key_proj = jnp.dot(hedge, w_key, preferred_element_type=jnp.float32)
    value_proj = jnp.dot(hedge, w_value, preferred_element_type=jnp.float32)
    query_feats = feature_map(query_proj).astype(jnp.bfloat16)
    key_feats = feature_map(key_proj).astype(jnp.bfloat16)
    value_rows = value_proj.astype(jnp.bfloat16)
    gram = jnp.dot(key_feats.T, value_rows, preferred_element_type=jnp.float32)
    key_total = jnp.sum(key_feats.astype(jnp.float32), axis=0)
    query_wide = query_feats.astype(jnp.float32)
    numer = jnp.dot(query_wide, gram, precision=lax.Precision.HIGHEST)
    denom = jnp.dot(query_wide, key_total, precision=lax.Precision.HIGHEST)
    attended = (numer / denom[:, None]).astype(jnp.bfloat16)
    mixed = hedge.astype(jnp.float32) + jnp.dot(attended, w_out, preferred_element_type=jnp.float32)
    return mixed.astype(jnp.bfloat16)
```

```python
import functools

import jax
import jax.numpy as jnp
from jax import lax
from jax.experimental import pallas as pl
from jax.experimental.pallas import tpu as pltpu
from jax.sharding import PartitionSpec as P

CORES = 2


def to_peer(index, step, count):
    if count & (count - 1) == 0:
        return index ^ step
    return (index + step) % count


def from_peer(index, step, count):
    if count & (count - 1) == 0:
        return index ^ step
    return (index + count - step) % count


def swap_cores(value):
    count = lax.axis_size("node")
    return lax.ppermute(value, "node", [(i, i ^ 1) for i in range(count)])


def send_edge(value, step):
    count = lax.axis_size("edge")
    return lax.ppermute(value, "edge", [(i, to_peer(i, step, count)) for i in range(count)])


def send_chip(value, step):
    chips = lax.axis_size("node") // CORES
    return lax.ppermute(
        value,
        "node",
        [(i, to_peer(i // CORES, step, chips) * CORES + i % CORES) for i in range(chips * CORES)],
    )


def vmem_call(kernel, outs, scratch=(), limit=16 * 2**20):
    def call(*args):
        spec = pl.BlockSpec(memory_space=pltpu.VMEM)
        return pl.pallas_call(
            kernel,
            out_shape=[pltpu.VMEM(shape, dtype) for shape, dtype in outs],
            in_specs=[spec] * len(args),
            out_specs=[spec] * len(outs),
            scratch_shapes=list(scratch),
            compiler_params=pltpu.CompilerParams(vmem_limit_bytes=limit),
        )(*[pltpu.with_memory_space_constraint(a, pltpu.VMEM) for a in args])

    return call


def feature_map(values):
    return jnp.where(values > 0, values + 1.0, jnp.exp(jnp.minimum(values, 0.0)))


def counts_kernel(chips, edges, owned, part, members, valid, members_other, valid_other, counts, columns):
    core = lax.axis_index("node") % CORES
    chip = lax.axis_index("node") // CORES
    edge = lax.axis_index("edge")
    slots = members.shape[0]
    own = jnp.where(valid[...] == 1, members[...], -1)
    other = jnp.where(valid_other[...] == 1, members_other[...], -1)
    columns[...] = jnp.concatenate([own, other], axis=0).T
    lanes = lax.broadcasted_iota(jnp.int32, (owned, part), 1)

    def chunk(step):
        owner = to_peer(chip, step, chips) * CORES + core
        rows = columns[pl.ds(pl.multiple_of(owner * owned, 8), owned), :]
        first = step * owned
        if not isinstance(first, int):
            first = pl.multiple_of(first, 8)
        for side in range(2):
            wanted = [rows[:, side * slots + s : side * slots + s + 1] for s in range(slots)]
            for block in range(edges):
                nodes = lanes + from_peer(edge, block, edges) * part
                total = jnp.zeros((owned, part), jnp.float32)
                for column in wanted:
                    total = total + jnp.where(column == nodes, 1.0, 0.0)
                place = (block * 2 + side) * part
                counts[pl.ds(first, owned), place : place + part] = total.astype(jnp.bfloat16)

    if chips <= 4:
        for step in range(chips):
            chunk(step)
    else:
        lax.fori_loop(0, chips, lambda step, _: chunk(step), None)


def aggregate_kernel(chips, edges, owned, counts, *refs):
    blocks, outs = refs[: 2 * edges], refs[2 * edges :]
    part = blocks[0].shape[0]
    group = min(chips, 4)
    for start in range(0, chips, group):
        total = None
        for block in range(edges):
            rows = jnp.concatenate([blocks[2 * block][...], blocks[2 * block + 1][...]], axis=0)
            term = jnp.dot(
                counts[start * owned : (start + group) * owned, block * 2 * part : (block + 1) * 2 * part],
                rows,
                preferred_element_type=jnp.float32,
            )
            total = term if total is None else total + term
        for step in range(group):
            out = outs[start + step]
            out[...] = total[step * owned : (step + 1) * owned].astype(out.dtype)


def hedge_kernel(scale, own, *refs):
    received, out = refs[:-1], refs[-1]
    total = own[...]
    for ref in received:
        total = total + ref[...].astype(jnp.float32)
    out[...] = (total / scale[:, :1]).astype(out.dtype)


def gram_kernel(edges, hedge, hedge_other, w_key, w_value, *outs):
    core = lax.axis_index("node") % CORES
    edge = lax.axis_index("edge")
    width = w_key.shape[0]
    half = width // CORES
    rows = half // edges
    both = jnp.concatenate([hedge[...], hedge_other[...]], axis=0)
    w_half = w_key[:, pl.ds(pl.multiple_of(core * half, 128), half)]
    keys = feature_map(jnp.dot(both, w_half, preferred_element_type=jnp.float32)).astype(jnp.bfloat16)
    values = jnp.dot(both, w_value[...], preferred_element_type=jnp.float32).astype(jnp.bfloat16)
    gram = outs[-1]
    gram[...] = lax.dot_general(
        keys, values, (((0,), (0,)), ((), ())), preferred_element_type=jnp.float32
    )
    key_sum = jnp.sum(keys.astype(jnp.float32), axis=0, keepdims=True)
    tail = jnp.concatenate([key_sum, jnp.zeros((1, width - half), jnp.float32)], axis=1)
    tail = jnp.broadcast_to(tail, (8, width))
    for step in range(edges):
        first = pl.multiple_of(to_peer(edge, step, edges) * rows, rows)
        piece = jnp.concatenate([gram[pl.ds(first, rows), :], tail], axis=0)
        outs[step][...] = piece.astype(outs[step].dtype)


def query_kernel(hedge, w_query, out):
    out[...] = feature_map(
        jnp.dot(hedge[...], w_query[...], preferred_element_type=jnp.float32)
    ).astype(out.dtype)


def add_kernel(own, *refs, count):
    received, outs = refs[:count], refs[count:]
    total = own[...]
    for ref in received:
        total = total + ref[...].astype(jnp.float32)
    for out in outs:
        out[...] = total[: out.shape[0]].astype(out.dtype)


def output_kernel(edges, query, hedge, w_out, *refs):
    pieces, out, gram = refs[: 2 * edges], refs[-2], refs[-1]
    core = lax.axis_index("node") % CORES
    edge = lax.axis_index("edge")
    width = w_out.shape[0]
    half = width // CORES
    rows = half // edges
    denom = None
    for side in range(2):
        base = (core if side == 0 else 1 - core) * half
        for step in range(edges):
            first = pl.multiple_of(base + from_peer(edge, step, edges) * rows, rows)
            gram[pl.ds(first, rows), :] = pieces[side * edges + step][:rows, :]
        key_sum = pieces[side * edges][rows : rows + 8, :][:1, :half].astype(jnp.float32)
        part = query[:, pl.ds(pl.multiple_of(base, 128), half)].astype(jnp.float32) * key_sum
        part = jnp.sum(part, axis=1, keepdims=True)
        denom = part if denom is None else denom + part
    numer = jnp.dot(query[...], gram[...], preferred_element_type=jnp.float32)
    attended = (numer / denom).astype(jnp.bfloat16)
    mixed = hedge[...].astype(jnp.float32) + jnp.dot(
        attended, w_out[...], preferred_element_type=jnp.float32
    )
    out[...] = mixed.astype(out.dtype)


def body(node_feats, members, incidence_mask, degrees, w_query, w_key, w_value, w_out):
    bf16, f32 = jnp.bfloat16, jnp.float32
    chips = lax.axis_size("node") // CORES
    edges = lax.axis_size("edge")
    part, width = node_feats.shape
    owned = degrees.shape[0]
    members, valid = members[0], incidence_mask[0]
    shard = members.shape[1]
    slots = members.shape[0]
    piece = width // CORES // edges + 8

    members_other, valid_other = swap_cores(members), swap_cores(valid)
    blocks = [node_feats] + [send_edge(node_feats, step) for step in range(1, edges)]
    paired = []
    for block in blocks:
        paired += [block, swap_cores(block)]
    scale = jnp.broadcast_to(jnp.maximum(degrees, 1).astype(f32)[:, None], (owned, 128))
    (counts,) = vmem_call(
        functools.partial(counts_kernel, chips, edges, owned, part),
        [((chips * owned, 2 * edges * part), bf16)],
        [pltpu.VMEM((shard, 2 * slots), jnp.int32)],
    )(members, valid, members_other, valid_other)
    partial = vmem_call(
        functools.partial(aggregate_kernel, chips, edges, owned),
        [((owned, width), f32)] + [((owned, width), bf16)] * (chips - 1),
    )(counts, *paired)
    arrived = [send_chip(partial[step], step) for step in range(1, chips)]
    (hedge,) = vmem_call(hedge_kernel, [((owned, width), bf16)])(scale, partial[0], *arrived)

    hedge_other = swap_cores(hedge)
    grams = vmem_call(
        functools.partial(gram_kernel, edges),
        [((piece, width), f32)] + [((piece, width), bf16)] * (edges - 1),
        [pltpu.VMEM((width // CORES, width), f32)],
    )(hedge, hedge_other, w_key, w_value)
    (query,) = vmem_call(query_kernel, [((owned, width), bf16)])(hedge, w_query)
    arrived = [send_edge(grams[step], step) for step in range(1, edges)]
    plane, plane16 = vmem_call(
        functools.partial(add_kernel, count=edges - 1),
        [((piece, width), f32), ((piece, width), bf16)],
    )(grams[0], *arrived)
    arrived = [send_chip(plane16, step) for step in range(1, chips)]
    whole, rows = vmem_call(
        functools.partial(add_kernel, count=chips - 1),
        [((piece, width), bf16), ((piece - 8, width), bf16)],
    )(plane, *arrived)
    pieces = [whole] + [send_edge(rows, step) for step in range(1, edges)]
    pieces += [swap_cores(value) for value in pieces]
    (mixed,) = vmem_call(
        functools.partial(output_kernel, edges),
        [((owned, width), bf16)],
        [pltpu.VMEM((width, width), bf16)],
    )(query, hedge, w_out, *pieces)
    return mixed


def solution(mesh):
    placed = (
        P(("node", "edge"), None),
        P("node", None, "edge"),
        P("node", None, "edge"),
        P(("edge", "node")),
        P(),
        P(),
        P(),
        P(),
    )
    return jax.shard_map(
        body, mesh=mesh, in_specs=placed, out_specs=P(("edge", "node"), None), check_vma=False
    )
```

```python
import functools

import jax
import jax.numpy as jnp
from jax import lax
from jax.experimental import pallas as pl
from jax.experimental.pallas import tpu as pltpu
from jax.sharding import PartitionSpec as P


VMEM_LIMIT = 16 * 2**20
CORES = 2


def to_peer(index, step, count):
    if count & (count - 1) == 0:
        return index ^ step
    return (index + step) % count


def from_peer(index, step, count):
    if count & (count - 1) == 0:
        return index ^ step
    return (index + count - step) % count


def swap_cores(value):
    count = lax.axis_size("node")
    return lax.ppermute(value, "node", [(i, i ^ 1) for i in range(count)])


def send_edge(value, step):
    count = lax.axis_size("edge")
    return lax.ppermute(value, "edge", [(i, to_peer(i, step, count)) for i in range(count)])


def send_chip(value, step):
    chips = lax.axis_size("node") // CORES
    return lax.ppermute(
        value,
        "node",
        [(i, to_peer(i // CORES, step, chips) * CORES + i % CORES) for i in range(chips * CORES)],
    )


def vmem_call(kernel, outs, scratch=()):
    def call(*args):
        spec = pl.BlockSpec(memory_space=pltpu.VMEM)
        return pl.pallas_call(
            kernel,
            out_shape=[pltpu.VMEM(shape, dtype) for shape, dtype in outs],
            in_specs=[spec] * len(args),
            out_specs=[spec] * len(outs),
            scratch_shapes=list(scratch),
            compiler_params=pltpu.CompilerParams(vmem_limit_bytes=VMEM_LIMIT),
        )(*[pltpu.with_memory_space_constraint(a, pltpu.VMEM) for a in args])

    return call


def preload_kernel(feats, members, valid, degrees, *refs):
    weights = (len(refs) - 6) // 2
    sources, feats_here, code = refs[:weights], refs[weights], refs[weights + 1]
    copies, (members_here, valid_here, degrees_here, sems) = refs[weights + 2 : -4], refs[-4:]
    moves = [
        pltpu.make_async_copy(source, target, sems.at[i])
        for i, (source, target) in enumerate(
            zip(
                (members, valid, degrees, feats) + tuple(sources),
                (members_here, valid_here, degrees_here, feats_here) + tuple(copies),
            )
        )
    ]
    for move in moves:
        move.start()
    for move in moves[:3]:
        move.wait()
    slots, owned = members.shape[0], degrees.shape[1]
    code[:slots, :] = jnp.where(valid_here[...] == 1, members_here[...], -1)
    code[slots : slots + 1, :owned] = degrees_here[...]
    for move in moves[3:]:
        move.wait()


def preload(feats, members, valid, degrees, *weights):
    args = (feats, members, valid, degrees) + weights
    outside = pl.BlockSpec(memory_space=pltpu.HBM)
    spec = pl.BlockSpec(memory_space=pltpu.VMEM)
    kept = [feats.shape, (2 * members.shape[0], members.shape[1])] + [w.shape for w in weights]
    kinds = [feats.dtype, members.dtype] + [w.dtype for w in weights]
    return pl.pallas_call(
        preload_kernel,
        out_shape=[pltpu.VMEM(shape, kind) for shape, kind in zip(kept, kinds)],
        in_specs=[outside] * len(args),
        out_specs=[spec] * len(kept),
        scratch_shapes=[
            pltpu.VMEM(members.shape, members.dtype),
            pltpu.VMEM(valid.shape, valid.dtype),
            pltpu.VMEM(degrees.shape, degrees.dtype),
            pltpu.SemaphoreType.DMA((len(args),)),
        ],
        compiler_params=pltpu.CompilerParams(vmem_limit_bytes=VMEM_LIMIT),
        name="preload",
    )(*[pltpu.with_memory_space_constraint(a, pltpu.HBM) for a in args])


def feature_map(values):
    return jnp.where(values > 0, values + 1.0, jnp.exp(jnp.minimum(values, 0.0)))


def half_place(half):
    core = lax.axis_index("node") % CORES
    mine = pl.ds(pl.multiple_of(core * half, half), half)
    other = pl.ds(pl.multiple_of((1 - core) * half, half), half)
    return mine, other


def pack_kernel(own, other, out):
    part, width = own.shape
    columns, _ = half_place(width // CORES)
    mine, theirs = half_place(part)
    out[mine, :] = own[:, columns]
    out[theirs, :] = other[:, columns]


def counts_kernel(chips, edges, owned, part, slots, code, code_other, counts, scale, columns):
    core = lax.axis_index("node") % CORES
    chip = lax.axis_index("node") // CORES
    edge = lax.axis_index("edge")
    first = jnp.where(core == 0, code[...], code_other[...])
    second = jnp.where(core == 0, code_other[...], code[...])
    columns[...] = jnp.concatenate([first, second], axis=0).T
    for side in range(CORES):
        place = side * 2 * slots + slots
        degree = jnp.maximum(columns[:owned, place : place + 1], 1).astype(jnp.float32)
        scale[side * owned : (side + 1) * owned, :] = jnp.broadcast_to(degree, (owned, scale.shape[1]))
    lanes = lax.broadcasted_iota(jnp.int32, (owned, part), 1)

    def chunk(step, turn):
        source = (to_peer(chip, step, chips) * CORES + turn) * owned
        rows = columns[pl.ds(pl.multiple_of(source, 8), owned), :]
        target = (step * CORES + turn) * owned
        if not isinstance(target, int):
            target = pl.multiple_of(target, 8)
        for side in range(CORES):
            base = side * 2 * slots
            wanted = [rows[:, base + s : base + s + 1] for s in range(slots)]
            for block in range(edges):
                nodes = lanes + from_peer(edge, block, edges) * part
                total = jnp.zeros((owned, part), jnp.float32)
                for column in wanted:
                    total = total + jnp.where(column == nodes, 1.0, 0.0)
                place = (block * CORES + side) * part
                counts[pl.ds(target, owned), place : place + part] = total.astype(jnp.bfloat16)

    if chips <= 4:
        for step in range(chips):
            for turn in range(CORES):
                chunk(step, turn)
    else:
        lax.fori_loop(0, chips * CORES, lambda i, _: chunk(i // CORES, i % CORES), None)


def aggregate_kernel(chips, edges, counts, *refs):
    blocks, outs = refs[:edges], refs[edges:]
    nodes = blocks[0].shape[0]
    rows = outs[0].shape[0]
    group = min(chips, 4)
    for start in range(0, chips, group):
        total = None
        for block in range(edges):
            term = jnp.dot(
                counts[start * rows : (start + group) * rows, block * nodes : (block + 1) * nodes],
                blocks[block][...],
                preferred_element_type=jnp.float32,
            )
            total = term if total is None else total + term
        for step in range(group):
            out = outs[start + step]
            out[...] = total[step * rows : (step + 1) * rows].astype(out.dtype)


def hedge_kernel(scale, own, *refs):
    received, out = refs[:-1], refs[-1]
    total = own[...]
    for ref in received:
        total = total + ref[...].astype(jnp.float32)
    out[...] = (total / scale[:, :1]).astype(out.dtype)


def gram_kernel(edges, hedge, hedge_other, w_key, w_value, *refs):
    outs, full, gram = refs[:edges], refs[edges], refs[edges + 1]
    edge = lax.axis_index("edge")
    width = w_key.shape[0]
    half = width // CORES
    rows = width // edges
    mine, other = half_place(half)
    full[:, mine] = hedge[...]
    full[:, other] = hedge_other[...]
    both = full[...]
    keys = feature_map(jnp.dot(both, w_key[...], preferred_element_type=jnp.float32)).astype(jnp.bfloat16)
    values = jnp.dot(both, w_value[:, mine], preferred_element_type=jnp.float32).astype(jnp.bfloat16)
    gram[...] = lax.dot_general(
        keys, values, (((0,), (0,)), ((), ())), preferred_element_type=jnp.float32
    )
    key_sum = jnp.sum(keys.astype(jnp.float32), axis=0, keepdims=True)
    tail = [key_sum[:, i * half : (i + 1) * half] for i in range(CORES)]
    tail = jnp.concatenate(tail + [jnp.zeros((8 - CORES, half), jnp.float32)], axis=0)
    for step in range(edges):
        first = pl.multiple_of(to_peer(edge, step, edges) * rows, rows)
        outs[step][:rows, :] = gram[pl.ds(first, rows), :].astype(outs[step].dtype)
        outs[step][rows:, :] = tail.astype(outs[step].dtype)


def query_kernel(full, w_query, out):
    out[...] = feature_map(
        jnp.dot(full[...], w_query[...], preferred_element_type=jnp.float32)
    ).astype(out.dtype)


def add_kernel(own, *refs, count):
    received, outs = refs[:count], refs[count:]
    total = own[...]
    for ref in received:
        total = total + ref[...].astype(jnp.float32)
    for out in outs:
        out[...] = total[: out.shape[0]].astype(out.dtype)


def denom_kernel(query, whole, out):
    half = whole.shape[1]
    tail = whole[whole.shape[0] - 8 :, :].astype(jnp.float32)
    denom = None
    for side in range(CORES):
        part = query[:, side * half : (side + 1) * half].astype(jnp.float32) * tail[side : side + 1, :]
        part = jnp.sum(part, axis=1, keepdims=True)
        denom = part if denom is None else denom + part
    out[...] = jnp.broadcast_to(denom, out.shape)


def attend_kernel(edges, query, denom, *refs):
    pieces, (mine, other, gram, attended) = refs[:edges], refs[edges:]
    edge = lax.axis_index("edge")
    rows = query.shape[1] // edges
    for step in range(edges):
        first = pl.multiple_of(from_peer(edge, step, edges) * rows, rows)
        gram[pl.ds(first, rows), :] = pieces[step][:rows, :]
    numer = jnp.dot(query[...], gram[...], preferred_element_type=jnp.float32)
    attended[...] = (numer / denom[:, :1]).astype(attended.dtype)
    here, there = half_place(mine.shape[0])
    mine[...] = attended[here, :]
    other[...] = attended[there, :]


def base_kernel(full, mine, w_out, out):
    here, _ = half_place(mine.shape[0])
    rows, _ = half_place(mine.shape[1])
    out[...] = full[here, :].astype(jnp.float32) + jnp.dot(
        mine[...], w_out[rows, :], preferred_element_type=jnp.float32
    )


def output_kernel(base, other, w_out, out, result, sems):
    _, rows = half_place(other.shape[1])
    half = other.shape[1]
    moves = []
    for side in range(CORES):
        place = pl.ds(side * half, half)
        mixed = base[:, place] + jnp.dot(
            other[...], w_out[rows, place], preferred_element_type=jnp.float32
        )
        result[:, place] = mixed.astype(result.dtype)
        moves.append(pltpu.make_async_copy(result.at[:, place], out.at[:, place], sems.at[side]))
        moves[-1].start()
    for move in moves:
        move.wait()


def write_output(base, other, w_out):
    args = (base, other, w_out)
    spec = pl.BlockSpec(memory_space=pltpu.VMEM)
    return pl.pallas_call(
        output_kernel,
        out_shape=pltpu.HBM(base.shape, other.dtype),
        in_specs=[spec] * len(args),
        out_specs=pl.BlockSpec(memory_space=pltpu.HBM),
        scratch_shapes=[
            pltpu.VMEM(base.shape, other.dtype),
            pltpu.SemaphoreType.DMA((CORES,)),
        ],
        compiler_params=pltpu.CompilerParams(vmem_limit_bytes=VMEM_LIMIT),
        name="output",
    )(*[pltpu.with_memory_space_constraint(a, pltpu.VMEM) for a in args])


def body(node_feats, members, incidence_mask, degrees, w_query, w_key, w_value, w_out):
    bf16, f32 = jnp.bfloat16, jnp.float32
    chips = lax.axis_size("node") // CORES
    edges = lax.axis_size("edge")
    part, width = node_feats.shape
    half = width // CORES
    owned = degrees.shape[0]
    pair = owned * CORES
    slots, shard = members.shape[1:]
    rows = width // edges
    piece = rows + 8

    feats_other = swap_cores(node_feats)
    feats, code, w_query, w_key, w_value, w_out = preload(
        node_feats, members[0], incidence_mask[0], degrees[None], w_query, w_key, w_value, w_out
    )
    (packed,) = vmem_call(pack_kernel, [((part * CORES, half), bf16)])(feats, feats_other)
    blocks = [packed] + [send_edge(packed, step) for step in range(1, edges)]
    code_other = swap_cores(code)
    counts, scale = vmem_call(
        functools.partial(counts_kernel, chips, edges, owned, part, slots),
        [((shard, CORES * edges * part), bf16), ((pair, 128), f32)],
        [pltpu.VMEM((shard, CORES * 2 * slots), jnp.int32)],
    )(code, code_other)
    partial = vmem_call(
        functools.partial(aggregate_kernel, chips, edges),
        [((pair, half), f32)] + [((pair, half), bf16)] * (chips - 1),
    )(counts, *blocks)
    arrived = [send_chip(partial[step], step) for step in range(1, chips)]
    (hedge,) = vmem_call(hedge_kernel, [((pair, half), bf16)])(scale, partial[0], *arrived)

    hedge_other = swap_cores(hedge)
    *grams, full = vmem_call(
        functools.partial(gram_kernel, edges),
        [((piece, half), f32)] + [((piece, half), bf16)] * (edges - 1) + [((pair, width), bf16)],
        [pltpu.VMEM((width, half), f32)],
    )(hedge, hedge_other, w_key, w_value)
    arrived = [send_edge(grams[step], step) for step in range(1, edges)]
    (query,) = vmem_call(query_kernel, [((pair, width), bf16)])(full, w_query)
    plane, plane16 = vmem_call(
        functools.partial(add_kernel, count=edges - 1),
        [((piece, half), f32), ((piece, half), bf16)],
    )(grams[0], *arrived)
    arrived = [send_chip(plane16, step) for step in range(1, chips)]
    whole, strip = vmem_call(
        functools.partial(add_kernel, count=chips - 1),
        [((piece, half), bf16), ((rows, half), bf16)],
    )(plane, *arrived)
    pieces = [whole] + [send_edge(strip, step) for step in range(1, edges)]
    (denom,) = vmem_call(denom_kernel, [((pair, 128), f32)])(query, whole)
    mine, other = vmem_call(
        functools.partial(attend_kernel, edges),
        [((owned, half), bf16)] * CORES,
        [pltpu.VMEM((width, half), bf16), pltpu.VMEM((pair, half), bf16)],
    )(query, denom, *pieces)
    arrived = swap_cores(other)
    (base,) = vmem_call(base_kernel, [((owned, width), f32)])(full, mine, w_out)
    return write_output(base, arrived, w_out)


def solution(mesh):
    placed = (
        P(("node", "edge"), None),
        P("node", None, "edge"),
        P("node", None, "edge"),
        P(("edge", "node")),
        P(),
        P(),
        P(),
        P(),
    )
    return jax.shard_map(
        body, mesh=mesh, in_specs=placed, out_specs=P(("edge", "node"), None), check_vma=False
    )
```

```python
import functools

import jax
import jax.numpy as jnp
from jax import lax
from jax.experimental import pallas as pl
from jax.experimental.pallas import tpu as pltpu
from jax.sharding import PartitionSpec as P


VMEM_LIMIT = 16 * 2**20
CORES = 2


def to_peer(index, step, count):
    if count & (count - 1) == 0:
        return index ^ step
    return (index + step) % count


def from_peer(index, step, count):
    if count & (count - 1) == 0:
        return index ^ step
    return (index + count - step) % count


def swap_cores(value):
    count = lax.axis_size("node")
    return lax.ppermute(value, "node", [(i, i ^ 1) for i in range(count)])


def send_edge(value, step):
    count = lax.axis_size("edge")
    return lax.ppermute(value, "edge", [(i, to_peer(i, step, count)) for i in range(count)])


def send_chip(value, step):
    chips = lax.axis_size("node") // CORES
    return lax.ppermute(
        value,
        "node",
        [(i, to_peer(i // CORES, step, chips) * CORES + i % CORES) for i in range(chips * CORES)],
    )


def vmem_call(kernel, outs, scratch=()):
    def call(*args):
        spec = pl.BlockSpec(memory_space=pltpu.VMEM)
        return pl.pallas_call(
            kernel,
            out_shape=[pltpu.VMEM(shape, dtype) for shape, dtype in outs],
            in_specs=[spec] * len(args),
            out_specs=[spec] * len(outs),
            scratch_shapes=list(scratch),
            compiler_params=pltpu.CompilerParams(vmem_limit_bytes=VMEM_LIMIT),
        )(*[pltpu.with_memory_space_constraint(a, pltpu.VMEM) for a in args])

    return call


def fetch_kernel(source, out, sem):
    move = pltpu.make_async_copy(source, out, sem)
    move.start()
    move.wait()


def fetch(value):
    return pl.pallas_call(
        fetch_kernel,
        out_shape=pltpu.VMEM(value.shape, value.dtype),
        in_specs=[pl.BlockSpec(memory_space=pltpu.HBM)],
        out_specs=pl.BlockSpec(memory_space=pltpu.VMEM),
        scratch_shapes=[pltpu.SemaphoreType.DMA],
        compiler_params=pltpu.CompilerParams(vmem_limit_bytes=VMEM_LIMIT),
        name="fetch",
    )(pltpu.with_memory_space_constraint(value, pltpu.HBM))


def preload_kernel(members, valid, degrees, *refs):
    weights = (len(refs) - 5) // 2
    sources, code = refs[:weights], refs[weights]
    copies, (members_here, valid_here, degrees_here, sems) = refs[weights + 1 : -4], refs[-4:]
    moves = [
        pltpu.make_async_copy(source, target, sems.at[i])
        for i, (source, target) in enumerate(
            zip(
                (members, valid, degrees) + tuple(sources),
                (members_here, valid_here, degrees_here) + tuple(copies),
            )
        )
    ]
    for move in moves:
        move.start()
    for move in moves[:3]:
        move.wait()
    slots, owned = members.shape[0], degrees.shape[1]
    code[:slots, :] = jnp.where(valid_here[...] == 1, members_here[...], -1)
    code[slots : slots + 1, :owned] = degrees_here[...]
    for move in moves[3:]:
        move.wait()


def preload(members, valid, degrees, *weights):
    args = (members, valid, degrees) + weights
    outside = pl.BlockSpec(memory_space=pltpu.HBM)
    spec = pl.BlockSpec(memory_space=pltpu.VMEM)
    kept = [(2 * members.shape[0], members.shape[1])] + [w.shape for w in weights]
    kinds = [members.dtype] + [w.dtype for w in weights]
    return pl.pallas_call(
        preload_kernel,
        out_shape=[pltpu.VMEM(shape, kind) for shape, kind in zip(kept, kinds)],
        in_specs=[outside] * len(args),
        out_specs=[spec] * len(kept),
        scratch_shapes=[
            pltpu.VMEM(members.shape, members.dtype),
            pltpu.VMEM(valid.shape, valid.dtype),
            pltpu.VMEM(degrees.shape, degrees.dtype),
            pltpu.SemaphoreType.DMA((len(args),)),
        ],
        compiler_params=pltpu.CompilerParams(vmem_limit_bytes=VMEM_LIMIT),
        name="preload",
    )(*[pltpu.with_memory_space_constraint(a, pltpu.HBM) for a in args])


def feature_map(values):
    return jnp.where(values > 0, values + 1.0, jnp.exp(jnp.minimum(values, 0.0)))


def half_place(half):
    core = lax.axis_index("node") % CORES
    mine = pl.ds(pl.multiple_of(core * half, half), half)
    other = pl.ds(pl.multiple_of((1 - core) * half, half), half)
    return mine, other


def pack_kernel(own, other, out):
    part, width = own.shape
    columns, _ = half_place(width // CORES)
    mine, theirs = half_place(part)
    out[mine, :] = own[:, columns]
    out[theirs, :] = other[:, columns]


def counts_kernel(chips, edges, owned, part, slots, code, code_other, counts, scale, columns):
    core = lax.axis_index("node") % CORES
    chip = lax.axis_index("node") // CORES
    edge = lax.axis_index("edge")
    first = jnp.where(core == 0, code[...], code_other[...])
    second = jnp.where(core == 0, code_other[...], code[...])
    columns[...] = jnp.concatenate([first, second], axis=0).T
    for side in range(CORES):
        place = side * 2 * slots + slots
        degree = jnp.maximum(columns[:owned, place : place + 1], 1).astype(jnp.float32)
        scale[side * owned : (side + 1) * owned, :] = jnp.broadcast_to(degree, (owned, scale.shape[1]))
    lanes = lax.broadcasted_iota(jnp.int32, (owned, part), 1)

    def chunk(step, turn):
        source = (to_peer(chip, step, chips) * CORES + turn) * owned
        rows = columns[pl.ds(pl.multiple_of(source, 8), owned), :]
        target = (step * CORES + turn) * owned
        if not isinstance(target, int):
            target = pl.multiple_of(target, 8)
        for side in range(CORES):
            base = side * 2 * slots
            wanted = [rows[:, base + s : base + s + 1] for s in range(slots)]
            for block in range(edges):
                nodes = lanes + from_peer(edge, block, edges) * part
                total = jnp.zeros((owned, part), jnp.float32)
                for column in wanted:
                    total = total + jnp.where(column == nodes, 1.0, 0.0)
                place = (block * CORES + side) * part
                counts[pl.ds(target, owned), place : place + part] = total.astype(jnp.bfloat16)

    if chips <= 4:
        for step in range(chips):
            for turn in range(CORES):
                chunk(step, turn)
    else:
        lax.fori_loop(0, chips * CORES, lambda i, _: chunk(i // CORES, i % CORES), None)


def blocks_sum(counts, place, blocks, used):
    nodes = blocks[0].shape[0]
    total = None
    for ref, block in zip(blocks, used):
        term = jnp.dot(
            counts[place, block * nodes : (block + 1) * nodes], ref[...], preferred_element_type=jnp.float32
        )
        total = term if total is None else total + term
    return total


def first_kernel(group, used, counts, *refs):
    blocks, out = refs[:-1], refs[-1]
    for start in range(0, out.shape[0], group):
        place = pl.ds(start, group)
        out[place, :] = blocks_sum(counts, place, blocks, used)


def aggregate_kernel(chips, used, counts, first, *refs):
    blocks, outs = refs[: len(used)], refs[len(used) :]
    rows = outs[0].shape[0]
    group = min(chips, 4)
    for start in range(0, chips, group):
        place = pl.ds(start * rows, group * rows)
        total = first[place, :] + blocks_sum(counts, place, blocks, used)
        for step in range(group):
            out = outs[start + step]
            out[...] = total[step * rows : (step + 1) * rows].astype(out.dtype)


def hedge_kernel(scale, own, *refs):
    received, out = refs[:-1], refs[-1]
    total = own[...]
    for ref in received:
        total = total + ref[...].astype(jnp.float32)
    out[...] = (total / scale[:, :1]).astype(out.dtype)


def project_kernel(hedge, w_key, w_value, key_part, value_part):
    mine, _ = half_place(hedge.shape[1])
    key_part[...] = jnp.dot(hedge[...], w_key[mine, :], preferred_element_type=jnp.float32)
    value_part[...] = jnp.dot(hedge[...], w_value[mine, mine], preferred_element_type=jnp.float32)


def gram_kernel(edges, hedge_other, key_part, value_part, w_key, w_value, *refs):
    outs, gram = refs[:edges], refs[edges]
    edge = lax.axis_index("edge")
    width = w_key.shape[0]
    half = width // CORES
    rows = width // edges
    mine, other = half_place(half)
    both = hedge_other[...]
    keys = key_part[...] + jnp.dot(both, w_key[other, :], preferred_element_type=jnp.float32)
    keys = feature_map(keys).astype(jnp.bfloat16)
    values = value_part[...] + jnp.dot(both, w_value[other, mine], preferred_element_type=jnp.float32)
    gram[...] = lax.dot_general(
        keys, values.astype(jnp.bfloat16), (((0,), (0,)), ((), ())), preferred_element_type=jnp.float32
    )
    key_sum = jnp.sum(keys.astype(jnp.float32), axis=0, keepdims=True)
    tail = [key_sum[:, i * half : (i + 1) * half] for i in range(CORES)]
    tail = jnp.concatenate(tail + [jnp.zeros((8 - CORES, half), jnp.float32)], axis=0)
    for step in range(edges):
        first = pl.multiple_of(to_peer(edge, step, edges) * rows, rows)
        outs[step][:rows, :] = gram[pl.ds(first, rows), :].astype(outs[step].dtype)
        outs[step][rows:, :] = tail.astype(outs[step].dtype)


def query_kernel(hedge, hedge_other, w_query, out, full):
    mine, other = half_place(hedge.shape[1])
    full[:, mine] = hedge[...]
    full[:, other] = hedge_other[...]
    out[...] = feature_map(
        jnp.dot(full[...], w_query[...], preferred_element_type=jnp.float32)
    ).astype(out.dtype)


def add_kernel(own, *refs, count):
    received, outs = refs[:count], refs[count:]
    total = own[...]
    for ref in received:
        total = total + ref[...].astype(jnp.float32)
    for out in outs:
        out[...] = total[: out.shape[0]].astype(out.dtype)


def numer_sum(edges, query, pieces, used):
    edge = lax.axis_index("edge")
    rows = query.shape[1] // edges
    total = None
    for ref, step in zip(pieces, used):
        place = pl.ds(pl.multiple_of(from_peer(edge, step, edges) * rows, 128), rows)
        term = jnp.dot(query[:, place], ref[:rows, :], preferred_element_type=jnp.float32)
        total = term if total is None else total + term
    return total


def denom_kernel(query, whole, out):
    half = whole.shape[1]
    tail = whole[whole.shape[0] - 8 :, :].astype(jnp.float32)
    denom = None
    for side in range(CORES):
        part = query[:, side * half : (side + 1) * half].astype(jnp.float32) * tail[side : side + 1, :]
        part = jnp.sum(part, axis=1, keepdims=True)
        denom = part if denom is None else denom + part
    out[...] = jnp.broadcast_to(denom, out.shape)


def numer_kernel(edges, used, query, *refs):
    refs[-1][...] = numer_sum(edges, query, refs[:-1], used)


def attend_kernel(edges, used, query, denom, numer, *refs):
    pieces, (mine, other, attended) = refs[: len(used)], refs[len(used) :]
    total = numer[...] + numer_sum(edges, query, pieces, used)
    attended[...] = (total / denom[:, :1]).astype(attended.dtype)
    split_rows(attended, mine, other)


def gather_kernel(edges, query, denom, *refs):
    pieces, (mine, other, attended, gram) = refs[:edges], refs[edges:]
    edge = lax.axis_index("edge")
    rows = query.shape[1] // edges
    for step in range(edges):
        first = pl.multiple_of(from_peer(edge, step, edges) * rows, rows)
        gram[pl.ds(first, rows), :] = pieces[step][:rows, :]
    numer = jnp.dot(query[...], gram[...], preferred_element_type=jnp.float32)
    attended[...] = (numer / denom[:, :1]).astype(attended.dtype)
    split_rows(attended, mine, other)


def split_rows(attended, mine, other):
    here, there = half_place(mine.shape[0])
    mine[...] = attended[here, :]
    other[...] = attended[there, :]


def base_kernel(full, mine, w_out, out):
    here, _ = half_place(mine.shape[0])
    rows, _ = half_place(mine.shape[1])
    out[...] = full[here, :].astype(jnp.float32) + jnp.dot(
        mine[...], w_out[rows, :], preferred_element_type=jnp.float32
    )


def output_kernel(base, other, w_out, out, result, sems):
    _, rows = half_place(other.shape[1])
    half = other.shape[1]
    moves = []
    for side in range(CORES):
        place = pl.ds(side * half, half)
        mixed = base[:, place] + jnp.dot(
            other[...], w_out[rows, place], preferred_element_type=jnp.float32
        )
        result[:, place] = mixed.astype(result.dtype)
        moves.append(pltpu.make_async_copy(result.at[:, place], out.at[:, place], sems.at[side]))
        moves[-1].start()
    for move in moves:
        move.wait()


def write_output(base, other, w_out):
    args = (base, other, w_out)
    spec = pl.BlockSpec(memory_space=pltpu.VMEM)
    return pl.pallas_call(
        output_kernel,
        out_shape=pltpu.HBM(base.shape, other.dtype),
        in_specs=[spec] * len(args),
        out_specs=pl.BlockSpec(memory_space=pltpu.HBM),
        scratch_shapes=[
            pltpu.VMEM(base.shape, other.dtype),
            pltpu.SemaphoreType.DMA((CORES,)),
        ],
        compiler_params=pltpu.CompilerParams(vmem_limit_bytes=VMEM_LIMIT),
        name="output",
    )(*[pltpu.with_memory_space_constraint(a, pltpu.VMEM) for a in args])


def body(node_feats, members, incidence_mask, degrees, w_query, w_key, w_value, w_out):
    bf16, f32 = jnp.bfloat16, jnp.float32
    chips = lax.axis_size("node") // CORES
    edges = lax.axis_size("edge")
    part, width = node_feats.shape
    half = width // CORES
    owned = degrees.shape[0]
    pair = owned * CORES
    slots, shard = members.shape[1:]
    rows = width // edges
    piece = rows + 8

    feats_other = swap_cores(node_feats)
    (packed,) = vmem_call(pack_kernel, [((part * CORES, half), bf16)])(
        fetch(node_feats), feats_other
    )
    blocks = [packed] + [send_edge(packed, step) for step in range(1, edges)]
    code, w_query, w_key, w_value, w_out = preload(
        members[0], incidence_mask[0], degrees[None], w_query, w_key, w_value, w_out
    )
    code_other = swap_cores(code)
    counts, scale = vmem_call(
        functools.partial(counts_kernel, chips, edges, owned, part, slots),
        [((shard, CORES * edges * part), bf16), ((pair, 128), f32)],
        [pltpu.VMEM((shard, CORES * 2 * slots), jnp.int32)],
    )(code, code_other)
    early, late = [0, edges - 1], list(range(1, edges - 1))
    (first,) = vmem_call(
        functools.partial(first_kernel, min(chips, 4) * pair, early), [((shard, half), f32)]
    )(counts, *[blocks[i] for i in early])
    partial = vmem_call(
        functools.partial(aggregate_kernel, chips, late), [((pair, half), f32)] + [((pair, half), bf16)] * (chips - 1)
    )(counts, first, *[blocks[i] for i in late])
    arrived = [send_chip(partial[step], step) for step in range(1, chips)]
    (hedge,) = vmem_call(hedge_kernel, [((pair, half), bf16)])(
        scale, partial[0], *arrived
    )

    hedge_other = swap_cores(hedge)
    parts = vmem_call(project_kernel, [((pair, width), f32), ((pair, half), f32)])(hedge, w_key, w_value)
    grams = vmem_call(
        functools.partial(gram_kernel, edges),
        [((piece, half), f32)] + [((piece, half), bf16)] * (edges - 1),
        [pltpu.VMEM((width, half), f32)],
    )(hedge_other, *parts, w_key, w_value)
    arrived = [send_edge(grams[step], step) for step in range(1, edges)]
    query, full = vmem_call(query_kernel, [((pair, width), bf16)] * 2)(
        hedge, hedge_other, w_query
    )
    plane, plane16 = vmem_call(
        functools.partial(add_kernel, count=edges - 1), [((piece, half), f32), ((piece, half), bf16)]
    )(grams[0], *arrived)
    arrived = [send_chip(plane16, step) for step in range(1, chips)]
    whole, strip = vmem_call(
        functools.partial(add_kernel, count=chips - 1), [((piece, half), bf16), ((rows, half), bf16)]
    )(plane, *arrived)
    pieces = [whole] + [send_edge(strip, step) for step in range(1, edges)]
    (denom,) = vmem_call(denom_kernel, [((pair, 128), f32)])(query, whole)
    halves, held = [((owned, half), bf16)] * CORES, pltpu.VMEM((pair, half), bf16)
    if rows % 128 == 0:
        (numer,) = vmem_call(
            functools.partial(numer_kernel, edges, early), [((pair, half), f32)]
        )(query, *[pieces[i] for i in early])
        mine, other = vmem_call(
            functools.partial(attend_kernel, edges, late), halves, [held]
        )(query, denom, numer, *[pieces[i] for i in late])
    else:
        mine, other = vmem_call(
            functools.partial(gather_kernel, edges), halves, [held, pltpu.VMEM((width, half), bf16)]
        )(query, denom, *pieces)
    arrived = swap_cores(other)
    (base,) = vmem_call(base_kernel, [((owned, width), f32)])(full, mine, w_out)
    return write_output(base, arrived, w_out)


def solution(mesh):
    placed = (
        P(("node", "edge"), None),
        P("node", None, "edge"),
        P("node", None, "edge"),
        P(("edge", "node")),
        P(),
        P(),
        P(),
        P(),
    )
    return jax.shard_map(body, mesh=mesh, in_specs=placed, out_specs=P(("edge", "node"), None), check_vma=False)
```

```python
import functools

import jax
import jax.numpy as jnp
from jax import lax
from jax.experimental import pallas as pl
from jax.experimental.pallas import tpu as pltpu
from jax.sharding import PartitionSpec as P


VMEM_LIMIT = 16 * 2**20

SENDS_FIRST = 1
CORES = 2


def to_peer(index, step, count):
    if count & (count - 1) == 0:
        return index ^ step
    return (index + step) % count


def from_peer(index, step, count):
    if count & (count - 1) == 0:
        return index ^ step
    return (index + count - step) % count


def swap_cores(value):
    count = lax.axis_size("node")
    return lax.ppermute(value, "node", [(i, i ^ 1) for i in range(count)])


def send_edge(value, step):
    count = lax.axis_size("edge")
    return lax.ppermute(value, "edge", [(i, to_peer(i, step, count)) for i in range(count)])


def send_chip(value, step):
    chips = lax.axis_size("node") // CORES
    return lax.ppermute(
        value,
        "node",
        [(i, to_peer(i // CORES, step, chips) * CORES + i % CORES) for i in range(chips * CORES)],
    )


def vmem_call(kernel, outs, scratch=()):
    def call(*args):
        spec = pl.BlockSpec(memory_space=pltpu.VMEM)
        return pl.pallas_call(
            kernel,
            out_shape=[pltpu.VMEM(shape, dtype) for shape, dtype in outs],
            in_specs=[spec] * len(args),
            out_specs=[spec] * len(outs),
            scratch_shapes=list(scratch),
            compiler_params=pltpu.CompilerParams(vmem_limit_bytes=VMEM_LIMIT),
        )(*[pltpu.with_memory_space_constraint(a, pltpu.VMEM) for a in args])

    return call


def fetch_kernel(source, out, sem):
    move = pltpu.make_async_copy(source, out, sem)
    move.start()
    move.wait()


def fetch(value):
    return pl.pallas_call(
        fetch_kernel,
        out_shape=pltpu.VMEM(value.shape, value.dtype),
        in_specs=[pl.BlockSpec(memory_space=pltpu.HBM)],
        out_specs=pl.BlockSpec(memory_space=pltpu.VMEM),
        scratch_shapes=[pltpu.SemaphoreType.DMA],
        compiler_params=pltpu.CompilerParams(vmem_limit_bytes=VMEM_LIMIT),
        name="fetch",
    )(pltpu.with_memory_space_constraint(value, pltpu.HBM))


def feature_map(values):
    return jnp.where(values > 0, values + 1.0, jnp.exp(jnp.minimum(values, 0.0)))


def half_place(half):
    core = lax.axis_index("node") % CORES
    mine = pl.ds(pl.multiple_of(core * half, half), half)
    other = pl.ds(pl.multiple_of((1 - core) * half, half), half)
    return mine, other


def pack_kernel(own, other, out):
    part, width = own.shape
    columns, _ = half_place(width // CORES)
    mine, theirs = half_place(part)
    out[mine, :] = own[:, columns]
    out[theirs, :] = other[:, columns]


def prepare_kernel(turn, chips, edges, owned, part, weights, *refs):
    members, valid, degrees, members_other, valid_other = refs[:5]
    sources, refs = refs[5 : 5 + weights], refs[5 + weights :]
    if len(refs) > 7 + weights:
        refs = refs[2 + weights :]
    counts, degree = refs[:2]
    copies, (members_here, valid_here, degrees_here, columns, sems) = refs[2 : 2 + weights], refs[2 + weights :]
    core = lax.axis_index("node") % CORES
    slots = members.shape[0]

    @pl.when(core == turn)
    def work():
        moves = [
            pltpu.make_async_copy(source, target, sems.at[i])
            for i, (source, target) in enumerate(
                zip(
                    (members, valid, degrees) + tuple(sources),
                    (members_here, valid_here, degrees_here) + tuple(copies),
                )
            )
        ]
        for move in moves:
            move.start()
        for move in moves[:3]:
            move.wait()
        degree[...] = jnp.ones(degree.shape, degree.dtype)
        degree[:1, :owned] = degrees_here[...]
        own = jnp.where(valid_here[...] == 1, members_here[...], -1)
        other = jnp.where(valid_other[...] == 1, members_other[...], -1)
        first = jnp.where(core == 0, own, other)
        second = jnp.where(core == 0, other, own)
        columns[...] = jnp.concatenate([first, second], axis=0).T
        build_counts(chips, edges, owned, part, slots, columns, counts)
        for move in moves[3:]:
            move.wait()


def build_counts(chips, edges, owned, part, slots, columns, counts):
    chip = lax.axis_index("node") // CORES
    edge = lax.axis_index("edge")
    lanes = lax.broadcasted_iota(jnp.int32, (owned, part), 1)

    def chunk(step, turn):
        source = (to_peer(chip, step, chips) * CORES + turn) * owned
        rows = columns[pl.ds(pl.multiple_of(source, 8), owned), :]
        target = (step * CORES + turn) * owned
        if not isinstance(target, int):
            target = pl.multiple_of(target, 8)
        for side in range(CORES):
            wanted = [rows[:, side * slots + s : side * slots + s + 1] for s in range(slots)]
            for block in range(edges):
                nodes = lanes + from_peer(edge, block, edges) * part
                total = jnp.zeros((owned, part), jnp.float32)
                for column in wanted:
                    total = total + jnp.where(column == nodes, 1.0, 0.0)
                place = (block * CORES + side) * part
                counts[pl.ds(target, owned), place : place + part] = total.astype(jnp.bfloat16)

    if chips <= 4:
        for step in range(chips):
            for turn in range(CORES):
                chunk(step, turn)
    else:
        lax.fori_loop(0, chips * CORES, lambda i, _: chunk(i // CORES, i % CORES), None)


def prepare(turn, sizes, held, members, valid, degrees, members_other, valid_other, *weights):
    chips, edges, owned, part = sizes
    slots, shard = members.shape
    shapes = [((shard, CORES * edges * part), jnp.bfloat16), ((8, 128), jnp.int32)]
    shapes += [(w.shape, w.dtype) for w in weights]
    outside, spec = pl.BlockSpec(memory_space=pltpu.HBM), pl.BlockSpec(memory_space=pltpu.VMEM)
    given = [pltpu.with_memory_space_constraint(a, pltpu.HBM) for a in (members, valid, degrees)]
    given += [pltpu.with_memory_space_constraint(a, pltpu.VMEM) for a in (members_other, valid_other)]
    given += [pltpu.with_memory_space_constraint(a, pltpu.HBM) for a in weights]
    specs = [outside] * 3 + [spec] * 2 + [outside] * len(weights)
    aliases = {len(given) + i: i for i in range(len(held))}
    given += [pltpu.with_memory_space_constraint(a, pltpu.VMEM) for a in held]
    specs += [spec] * len(held)
    return pl.pallas_call(
        functools.partial(prepare_kernel, turn, chips, edges, owned, part, len(weights)),
        out_shape=[pltpu.VMEM(shape, kind) for shape, kind in shapes],
        in_specs=specs,
        out_specs=[spec] * len(shapes),
        scratch_shapes=[
            pltpu.VMEM(members.shape, members.dtype),
            pltpu.VMEM(valid.shape, valid.dtype),
            pltpu.VMEM(degrees.shape, degrees.dtype),
            pltpu.VMEM((shard, CORES * slots), jnp.int32),
            pltpu.SemaphoreType.DMA((3 + len(weights),)),
        ],
        input_output_aliases=aliases,
        compiler_params=pltpu.CompilerParams(vmem_limit_bytes=VMEM_LIMIT),
    )(*given)


def scale_kernel(degree, degree_other, scale):
    core = lax.axis_index("node") % CORES
    owned = scale.shape[0] // CORES
    for here, ref in ((core, degree), (1 - core, degree_other)):
        line = jnp.maximum(ref[:1, :], 1).astype(jnp.float32)
        column = jnp.broadcast_to(line, (128, 128)).T
        scale[pl.ds(pl.multiple_of(here * owned, 8), owned), :] = column[:owned, :]


def blocks_sum(counts, place, blocks, used):
    nodes = blocks[0].shape[0]
    total = None
    for ref, block in zip(blocks, used):
        term = jnp.dot(
            counts[place, block * nodes : (block + 1) * nodes], ref[...], preferred_element_type=jnp.float32
        )
        total = term if total is None else total + term
    return total


def first_kernel(group, used, counts, *refs):
    blocks, out = refs[:-1], refs[-1]
    for start in range(0, out.shape[0], group):
        place = pl.ds(start, group)
        out[place, :] = blocks_sum(counts, place, blocks, used)


def aggregate_kernel(chips, used, counts, first, *refs):
    blocks, outs = refs[: len(used)], refs[len(used) :]
    rows = outs[0].shape[0]
    group = min(chips, 4)
    for start in range(0, chips, group):
        place = pl.ds(start * rows, group * rows)
        total = first[place, :] + blocks_sum(counts, place, blocks, used)
        for step in range(group):
            out = outs[start + step]
            out[...] = total[step * rows : (step + 1) * rows].astype(out.dtype)


def hedge_kernel(scale, own, *refs):
    received, out = refs[:-1], refs[-1]
    total = own[...]
    for ref in received:
        total = total + ref[...].astype(jnp.float32)
    out[...] = (total / scale[:, :1]).astype(out.dtype)


def project_kernel(hedge, w_key, w_value, key_part, value_part):
    mine, _ = half_place(hedge.shape[1])
    key_part[...] = jnp.dot(hedge[...], w_key[mine, :], preferred_element_type=jnp.float32)
    value_part[...] = jnp.dot(hedge[...], w_value[mine, mine], preferred_element_type=jnp.float32)


def gram_kernel(edges, hedge_other, key_part, value_part, w_key, w_value, *refs):
    outs, gram = refs[:edges], refs[edges]
    edge = lax.axis_index("edge")
    width = w_key.shape[0]
    half = width // CORES
    rows = width // edges
    mine, other = half_place(half)
    both = hedge_other[...]
    keys = key_part[...] + jnp.dot(both, w_key[other, :], preferred_element_type=jnp.float32)
    keys = feature_map(keys).astype(jnp.bfloat16)
    values = value_part[...] + jnp.dot(both, w_value[other, mine], preferred_element_type=jnp.float32)
    gram[...] = lax.dot_general(
        keys, values.astype(jnp.bfloat16), (((0,), (0,)), ((), ())), preferred_element_type=jnp.float32
    )
    key_sum = jnp.sum(keys.astype(jnp.float32), axis=0, keepdims=True)
    tail = [key_sum[:, i * half : (i + 1) * half] for i in range(CORES)]
    tail = jnp.concatenate(tail + [jnp.zeros((8 - CORES, half), jnp.float32)], axis=0)
    for step in range(edges):
        first = pl.multiple_of(to_peer(edge, step, edges) * rows, rows)
        outs[step][:rows, :] = gram[pl.ds(first, rows), :].astype(outs[step].dtype)
        outs[step][rows:, :] = tail.astype(outs[step].dtype)


def query_kernel(hedge, hedge_other, w_query, out, full):
    mine, other = half_place(hedge.shape[1])
    full[:, mine] = hedge[...]
    full[:, other] = hedge_other[...]
    out[...] = feature_map(
        jnp.dot(full[...], w_query[...], preferred_element_type=jnp.float32)
    ).astype(out.dtype)


def add_kernel(own, *refs, count):
    received, outs = refs[:count], refs[count:]
    total = own[...]
    for ref in received:
        total = total + ref[...].astype(jnp.float32)
    for out in outs:
        out[...] = total[: out.shape[0]].astype(out.dtype)


def numer_sum(edges, query, pieces, used):
    edge = lax.axis_index("edge")
    rows = query.shape[1] // edges
    total = None
    for ref, step in zip(pieces, used):
        place = pl.ds(pl.multiple_of(from_peer(edge, step, edges) * rows, 128), rows)
        term = jnp.dot(query[:, place], ref[:rows, :], preferred_element_type=jnp.float32)
        total = term if total is None else total + term
    return total


def denom_kernel(query, whole, out):
    half = whole.shape[1]
    tail = whole[whole.shape[0] - 8 :, :].astype(jnp.float32)
    denom = None
    for side in range(CORES):
        part = query[:, side * half : (side + 1) * half].astype(jnp.float32) * tail[side : side + 1, :]
        part = jnp.sum(part, axis=1, keepdims=True)
        denom = part if denom is None else denom + part
    out[...] = jnp.broadcast_to(denom, out.shape)


def numer_kernel(edges, used, query, *refs):
    refs[-1][...] = numer_sum(edges, query, refs[:-1], used)


def attend_kernel(edges, used, query, denom, numer, *refs):
    pieces, (mine, other, attended) = refs[: len(used)], refs[len(used) :]
    total = numer[...] + numer_sum(edges, query, pieces, used)
    attended[...] = (total / denom[:, :1]).astype(attended.dtype)
    split_rows(attended, mine, other)


def gather_kernel(edges, query, denom, *refs):
    pieces, (mine, other, attended, gram) = refs[:edges], refs[edges:]
    edge = lax.axis_index("edge")
    rows = query.shape[1] // edges
    for step in range(edges):
        first = pl.multiple_of(from_peer(edge, step, edges) * rows, rows)
        gram[pl.ds(first, rows), :] = pieces[step][:rows, :]
    numer = jnp.dot(query[...], gram[...], preferred_element_type=jnp.float32)
    attended[...] = (numer / denom[:, :1]).astype(attended.dtype)
    split_rows(attended, mine, other)


def split_rows(attended, mine, other):
    here, there = half_place(mine.shape[0])
    mine[...] = attended[here, :]
    other[...] = attended[there, :]


def base_kernel(full, mine, w_out, out):
    here, _ = half_place(mine.shape[0])
    rows, _ = half_place(mine.shape[1])
    out[...] = full[here, :].astype(jnp.float32) + jnp.dot(
        mine[...], w_out[rows, :], preferred_element_type=jnp.float32
    )


def output_kernel(base, other, w_out, out, result, sems):
    _, rows = half_place(other.shape[1])
    half = other.shape[1]
    moves = []
    for side in range(CORES):
        place = pl.ds(side * half, half)
        mixed = base[:, place] + jnp.dot(
            other[...], w_out[rows, place], preferred_element_type=jnp.float32
        )
        result[:, place] = mixed.astype(result.dtype)
        moves.append(pltpu.make_async_copy(result.at[:, place], out.at[:, place], sems.at[side]))
        moves[-1].start()
    for move in moves:
        move.wait()


def write_output(base, other, w_out):
    args = (base, other, w_out)
    spec = pl.BlockSpec(memory_space=pltpu.VMEM)
    return pl.pallas_call(
        output_kernel,
        out_shape=pltpu.HBM(base.shape, other.dtype),
        in_specs=[spec] * len(args),
        out_specs=pl.BlockSpec(memory_space=pltpu.HBM),
        scratch_shapes=[
            pltpu.VMEM(base.shape, other.dtype),
            pltpu.SemaphoreType.DMA((CORES,)),
        ],
        compiler_params=pltpu.CompilerParams(vmem_limit_bytes=VMEM_LIMIT),
        name="output",
    )(*[pltpu.with_memory_space_constraint(a, pltpu.VMEM) for a in args])


def body(node_feats, members, incidence_mask, degrees, w_query, w_key, w_value, w_out):
    bf16, f32 = jnp.bfloat16, jnp.float32
    chips = lax.axis_size("node") // CORES
    edges = lax.axis_size("edge")
    part, width = node_feats.shape
    half = width // CORES
    owned = degrees.shape[0]
    pair = owned * CORES
    _, shard = members.shape[1:]
    rows = width // edges
    piece = rows + 8

    feats_other = swap_cores(node_feats)
    (packed,) = vmem_call(pack_kernel, [((part * CORES, half), bf16)])(
        fetch(node_feats), feats_other
    )
    blocks = [packed] + [send_edge(packed, step) for step in range(1, edges)]
    weights = (w_query, w_key, w_value, w_out)
    sizes = (chips, edges, owned, part)
    given = (members[0], incidence_mask[0], degrees[None])
    given += (swap_cores(given[0]), swap_cores(given[1])) + weights
    held = prepare(1 - SENDS_FIRST, sizes, (), *given)
    counts, degree, w_query, w_key, w_value, w_out = prepare(SENDS_FIRST, sizes, held, *given)
    early, late = [0, edges - 1], list(range(1, edges - 1))
    (first,) = vmem_call(
        functools.partial(first_kernel, min(chips, 4) * pair, early), [((shard, half), f32)]
    )(counts, *[blocks[i] for i in early])
    partial = vmem_call(
        functools.partial(aggregate_kernel, chips, late), [((pair, half), f32)] + [((pair, half), bf16)] * (chips - 1)
    )(counts, first, *[blocks[i] for i in late])
    arrived = [send_chip(partial[step], step) for step in range(1, chips)]
    (scale,) = vmem_call(scale_kernel, [((pair, 128), f32)])(degree, swap_cores(degree))
    (hedge,) = vmem_call(hedge_kernel, [((pair, half), bf16)])(
        scale, partial[0], *arrived
    )

    hedge_other = swap_cores(hedge)
    parts = vmem_call(project_kernel, [((pair, width), f32), ((pair, half), f32)])(hedge, w_key, w_value)
    grams = vmem_call(
        functools.partial(gram_kernel, edges),
        [((piece, half), f32)] + [((piece, half), bf16)] * (edges - 1),
        [pltpu.VMEM((width, half), f32)],
    )(hedge_other, *parts, w_key, w_value)
    arrived = [send_edge(grams[step], step) for step in range(1, edges)]
    query, full = vmem_call(query_kernel, [((pair, width), bf16)] * 2)(
        hedge, hedge_other, w_query
    )
    plane, plane16 = vmem_call(
        functools.partial(add_kernel, count=edges - 1), [((piece, half), f32), ((piece, half), bf16)]
    )(grams[0], *arrived)
    arrived = [send_chip(plane16, step) for step in range(1, chips)]
    whole, strip = vmem_call(
        functools.partial(add_kernel, count=chips - 1), [((piece, half), bf16), ((rows, half), bf16)]
    )(plane, *arrived)
    pieces = [whole] + [send_edge(strip, step) for step in range(1, edges)]
    (denom,) = vmem_call(denom_kernel, [((pair, 128), f32)])(query, whole)
    halves, held = [((owned, half), bf16)] * CORES, pltpu.VMEM((pair, half), bf16)
    if rows % 128 == 0:
        (numer,) = vmem_call(
            functools.partial(numer_kernel, edges, early), [((pair, half), f32)]
        )(query, *[pieces[i] for i in early])
        mine, other = vmem_call(
            functools.partial(attend_kernel, edges, late), halves, [held]
        )(query, denom, numer, *[pieces[i] for i in late])
    else:
        mine, other = vmem_call(
            functools.partial(gather_kernel, edges), halves, [held, pltpu.VMEM((width, half), bf16)]
        )(query, denom, *pieces)
    arrived = swap_cores(other)
    (base,) = vmem_call(base_kernel, [((owned, width), f32)])(full, mine, w_out)
    return write_output(base, arrived, w_out)


def solution(mesh):
    placed = (
        P(("node", "edge"), None),
        P("node", None, "edge"),
        P("node", None, "edge"),
        P(("edge", "node")),
        P(),
        P(),
        P(),
        P(),
    )
    return jax.shard_map(body, mesh=mesh, in_specs=placed, out_specs=P(("edge", "node"), None), check_vma=False)
```

```python
import functools

import jax
import jax.numpy as jnp
from jax import lax
from jax.experimental import pallas as pl
from jax.experimental.pallas import tpu as pltpu
from jax.sharding import PartitionSpec as P


VMEM_LIMIT = 16 * 2**20

SENDS_FIRST = 1
CORES = 2


def to_peer(index, step, count):
    if count & (count - 1) == 0:
        return index ^ step
    return (index + step) % count


def from_peer(index, step, count):
    if count & (count - 1) == 0:
        return index ^ step
    return (index + count - step) % count


def swap_cores(value):
    count = lax.axis_size("node")
    return lax.ppermute(value, "node", [(i, i ^ 1) for i in range(count)])


def send_edge(value, step):
    count = lax.axis_size("edge")
    return lax.ppermute(value, "edge", [(i, to_peer(i, step, count)) for i in range(count)])


def send_chip(value, step):
    chips = lax.axis_size("node") // CORES
    return lax.ppermute(
        value,
        "node",
        [(i, to_peer(i // CORES, step, chips) * CORES + i % CORES) for i in range(chips * CORES)],
    )


def vmem_call(kernel, outs, scratch=()):
    def call(*args):
        spec = pl.BlockSpec(memory_space=pltpu.VMEM)
        return pl.pallas_call(
            kernel,
            out_shape=[pltpu.VMEM(shape, dtype) for shape, dtype in outs],
            in_specs=[spec] * len(args),
            out_specs=[spec] * len(outs),
            scratch_shapes=list(scratch),
            compiler_params=pltpu.CompilerParams(vmem_limit_bytes=VMEM_LIMIT),
        )(*[pltpu.with_memory_space_constraint(a, pltpu.VMEM) for a in args])

    return call


def fetch_kernel(source, out, sem):
    move = pltpu.make_async_copy(source, out, sem)
    move.start()
    move.wait()


def fetch(value):
    return pl.pallas_call(
        fetch_kernel,
        out_shape=pltpu.VMEM(value.shape, value.dtype),
        in_specs=[pl.BlockSpec(memory_space=pltpu.HBM)],
        out_specs=pl.BlockSpec(memory_space=pltpu.VMEM),
        scratch_shapes=[pltpu.SemaphoreType.DMA],
        compiler_params=pltpu.CompilerParams(vmem_limit_bytes=VMEM_LIMIT),
        name="fetch",
    )(pltpu.with_memory_space_constraint(value, pltpu.HBM))


def feature_map(values):
    return jnp.where(values > 0, values + 1.0, jnp.exp(jnp.minimum(values, 0.0)))


def half_place(half):
    core = lax.axis_index("node") % CORES
    mine = pl.ds(pl.multiple_of(core * half, half), half)
    other = pl.ds(pl.multiple_of((1 - core) * half, half), half)
    return mine, other


def pack_kernel(own, other, out):
    part, width = own.shape
    columns, _ = half_place(width // CORES)
    mine, theirs = half_place(part)
    out[mine, :] = own[:, columns]
    out[theirs, :] = other[:, columns]


def prepare_kernel(turn, chips, edges, owned, part, weights, *refs):
    members, valid, degrees, members_other, valid_other = refs[:5]
    sources, refs = refs[5 : 5 + weights], refs[5 + weights :]
    if len(refs) > 7 + weights:
        refs = refs[2 + weights :]
    counts, degree = refs[:2]
    copies, (members_here, valid_here, degrees_here, columns, sems) = refs[2 : 2 + weights], refs[2 + weights :]
    core = lax.axis_index("node") % CORES
    slots = members.shape[0]

    @pl.when(core == turn)
    def work():
        moves = [
            pltpu.make_async_copy(source, target, sems.at[i])
            for i, (source, target) in enumerate(
                zip(
                    (members, valid, degrees) + tuple(sources),
                    (members_here, valid_here, degrees_here) + tuple(copies),
                )
            )
        ]
        for move in moves:
            move.start()
        for move in moves[:3]:
            move.wait()
        degree[...] = jnp.ones(degree.shape, degree.dtype)
        degree[:1, :owned] = degrees_here[...]
        own = jnp.where(valid_here[...] == 1, members_here[...], -1)
        other = jnp.where(valid_other[...] == 1, members_other[...], -1)
        first = jnp.where(core == 0, own, other)
        second = jnp.where(core == 0, other, own)
        columns[...] = jnp.concatenate([first, second], axis=0).T
        build_counts(chips, edges, owned, part, slots, columns, counts)
        for move in moves[3:]:
            move.wait()


def build_counts(chips, edges, owned, part, slots, columns, counts):
    chip = lax.axis_index("node") // CORES
    edge = lax.axis_index("edge")
    lanes = lax.broadcasted_iota(jnp.int32, (owned, part), 1)

    def chunk(step, turn):
        source = (to_peer(chip, step, chips) * CORES + turn) * owned
        rows = columns[pl.ds(pl.multiple_of(source, 8), owned), :]
        target = (step * CORES + turn) * owned
        if not isinstance(target, int):
            target = pl.multiple_of(target, 8)
        for side in range(CORES):
            wanted = [rows[:, side * slots + s : side * slots + s + 1] for s in range(slots)]
            for block in range(edges):
                nodes = lanes + from_peer(edge, block, edges) * part
                total = jnp.zeros((owned, part), jnp.float32)
                for column in wanted:
                    total = total + jnp.where(column == nodes, 1.0, 0.0)
                place = (block * CORES + side) * part
                counts[pl.ds(target, owned), place : place + part] = total.astype(jnp.bfloat16)

    if chips <= 4:
        for step in range(chips):
            for turn in range(CORES):
                chunk(step, turn)
    else:
        lax.fori_loop(0, chips * CORES, lambda i, _: chunk(i // CORES, i % CORES), None)


def prepare(turn, sizes, held, members, valid, degrees, members_other, valid_other, *weights):
    chips, edges, owned, part = sizes
    slots, shard = members.shape
    shapes = [((shard, CORES * edges * part), jnp.bfloat16), ((8, 128), jnp.int32)]
    shapes += [(w.shape, w.dtype) for w in weights]
    outside, spec = pl.BlockSpec(memory_space=pltpu.HBM), pl.BlockSpec(memory_space=pltpu.VMEM)
    given = [pltpu.with_memory_space_constraint(a, pltpu.HBM) for a in (members, valid, degrees)]
    given += [pltpu.with_memory_space_constraint(a, pltpu.VMEM) for a in (members_other, valid_other)]
    given += [pltpu.with_memory_space_constraint(a, pltpu.HBM) for a in weights]
    specs = [outside] * 3 + [spec] * 2 + [outside] * len(weights)
    aliases = {len(given) + i: i for i in range(len(held))}
    given += [pltpu.with_memory_space_constraint(a, pltpu.VMEM) for a in held]
    specs += [spec] * len(held)
    return pl.pallas_call(
        functools.partial(prepare_kernel, turn, chips, edges, owned, part, len(weights)),
        out_shape=[pltpu.VMEM(shape, kind) for shape, kind in shapes],
        in_specs=specs,
        out_specs=[spec] * len(shapes),
        scratch_shapes=[
            pltpu.VMEM(members.shape, members.dtype),
            pltpu.VMEM(valid.shape, valid.dtype),
            pltpu.VMEM(degrees.shape, degrees.dtype),
            pltpu.VMEM((shard, CORES * slots), jnp.int32),
            pltpu.SemaphoreType.DMA((3 + len(weights),)),
        ],
        input_output_aliases=aliases,
        compiler_params=pltpu.CompilerParams(vmem_limit_bytes=VMEM_LIMIT),
    )(*given)


def scale_kernel(degree, degree_other, scale):
    core = lax.axis_index("node") % CORES
    owned = scale.shape[0] // CORES
    for here, ref in ((core, degree), (1 - core, degree_other)):
        line = jnp.maximum(ref[:1, :], 1).astype(jnp.float32)
        column = jnp.broadcast_to(line, (128, 128)).T
        scale[pl.ds(pl.multiple_of(here * owned, 8), owned), :] = column[:owned, :]


def blocks_sum(counts, place, blocks, used):
    nodes = blocks[0].shape[0]
    total = None
    for ref, block in zip(blocks, used):
        term = jnp.dot(
            counts[place, block * nodes : (block + 1) * nodes], ref[...], preferred_element_type=jnp.float32
        )
        total = term if total is None else total + term
    return total


def first_kernel(group, used, counts, *refs):
    blocks, out = refs[:-1], refs[-1]
    for start in range(0, out.shape[0], group):
        place = pl.ds(start, group)
        out[place, :] = blocks_sum(counts, place, blocks, used)


def aggregate_kernel(chips, used, counts, first, *refs):
    blocks, outs = refs[: len(used)], refs[len(used) :]
    rows = outs[0].shape[0]
    group = min(chips, 4)
    for start in range(0, chips, group):
        place = pl.ds(start * rows, group * rows)
        total = first[place, :] + blocks_sum(counts, place, blocks, used)
        for step in range(group):
            out = outs[start + step]
            out[...] = total[step * rows : (step + 1) * rows].astype(out.dtype)


def hedge_kernel(scale, own, *refs):
    received, out = refs[:-1], refs[-1]
    total = own[...]
    for ref in received:
        total = total + ref[...].astype(jnp.float32)
    out[...] = (total / scale[:, :1]).astype(out.dtype)


def fold_kernel(w_value, w_out, folded):
    mine, _ = half_place(folded.shape[1])
    folded[...] = jnp.dot(w_value[...], w_out[:, mine], preferred_element_type=jnp.float32).astype(
        folded.dtype
    )


def project_kernel(hedge, w_key, folded, key_part, value_part):
    mine, _ = half_place(hedge.shape[1])
    key_part[...] = jnp.dot(hedge[...], w_key[mine, :], preferred_element_type=jnp.float32)
    value_part[...] = jnp.dot(hedge[...], folded[mine, :], preferred_element_type=jnp.float32)


def gram_kernel(edges, hedge_other, key_part, value_part, w_key, folded, *refs):
    outs, gram = refs[:edges], refs[edges]
    edge = lax.axis_index("edge")
    width = w_key.shape[0]
    half = width // CORES
    rows = width // edges
    _, other = half_place(half)
    both = hedge_other[...]
    keys = key_part[...] + jnp.dot(both, w_key[other, :], preferred_element_type=jnp.float32)
    keys = feature_map(keys).astype(jnp.bfloat16)
    values = value_part[...] + jnp.dot(both, folded[other, :], preferred_element_type=jnp.float32)
    gram[...] = lax.dot_general(
        keys, values.astype(jnp.bfloat16), (((0,), (0,)), ((), ())), preferred_element_type=jnp.float32
    )
    key_sum = jnp.sum(keys.astype(jnp.float32), axis=0, keepdims=True)
    tail = [key_sum[:, i * half : (i + 1) * half] for i in range(CORES)]
    tail = jnp.concatenate(tail + [jnp.zeros((8 - CORES, half), jnp.float32)], axis=0)
    for step in range(edges):
        first = pl.multiple_of(to_peer(edge, step, edges) * rows, rows)
        outs[step][:rows, :] = gram[pl.ds(first, rows), :].astype(outs[step].dtype)
        outs[step][rows:, :] = tail.astype(outs[step].dtype)


def query_kernel(hedge, hedge_other, w_query, out):
    mine, other = half_place(hedge.shape[1])
    total = jnp.dot(hedge[...], w_query[mine, :], preferred_element_type=jnp.float32)
    total = total + jnp.dot(hedge_other[...], w_query[other, :], preferred_element_type=jnp.float32)
    out[...] = feature_map(total).astype(out.dtype)


def add_kernel(own, *refs, count):
    received, outs = refs[:count], refs[count:]
    total = own[...]
    for ref in received:
        total = total + ref[...].astype(jnp.float32)
    for out in outs:
        out[...] = total[: out.shape[0]].astype(out.dtype)


def numer_sum(edges, query, pieces, used):
    edge = lax.axis_index("edge")
    rows = query.shape[1] // edges
    total = None
    for ref, step in zip(pieces, used):
        place = pl.ds(pl.multiple_of(from_peer(edge, step, edges) * rows, 128), rows)
        term = jnp.dot(query[:, place], ref[:rows, :], preferred_element_type=jnp.float32)
        total = term if total is None else total + term
    return total


def denom_kernel(query, whole, out):
    half = whole.shape[1]
    tail = whole[whole.shape[0] - 8 :, :].astype(jnp.float32)
    denom = None
    for side in range(CORES):
        part = query[:, side * half : (side + 1) * half].astype(jnp.float32) * tail[side : side + 1, :]
        part = jnp.sum(part, axis=1, keepdims=True)
        denom = part if denom is None else denom + part
    out[...] = jnp.broadcast_to(denom, out.shape)


def numer_kernel(edges, used, query, *refs):
    refs[-1][...] = numer_sum(edges, query, refs[:-1], used)


def attend_kernel(edges, used, hedge, query, denom, numer, *refs):
    pieces, (mine, other, mixed) = refs[: len(used)], refs[len(used) :]
    total = numer[...] + numer_sum(edges, query, pieces, used)
    mix_rows(hedge, total / denom[:, :1], mixed, mine, other)


def gather_kernel(edges, hedge, query, denom, *refs):
    pieces, (mine, other, mixed, gram) = refs[:edges], refs[edges:]
    edge = lax.axis_index("edge")
    rows = query.shape[1] // edges
    for step in range(edges):
        first = pl.multiple_of(from_peer(edge, step, edges) * rows, rows)
        gram[pl.ds(first, rows), :] = pieces[step][:rows, :]
    numer = jnp.dot(query[...], gram[...], preferred_element_type=jnp.float32)
    mix_rows(hedge, numer / denom[:, :1], mixed, mine, other)


def mix_rows(hedge, attended, mixed, mine, other):
    mixed[...] = (hedge[...].astype(jnp.float32) + attended).astype(mixed.dtype)
    here, there = half_place(mine.shape[0])
    mine[...] = mixed[here, :]
    other[...] = mixed[there, :]


def store_kernel(side, value, *refs):
    out, sem = refs[-2:]
    move = pltpu.make_async_copy(value, out.at[:, half_place(value.shape[1])[side]], sem)
    move.start()
    move.wait()


def store(side, value, *held):
    outside = pl.BlockSpec(memory_space=pltpu.HBM)
    return pl.pallas_call(
        functools.partial(store_kernel, side),
        out_shape=pltpu.HBM((value.shape[0], CORES * value.shape[1]), value.dtype),
        in_specs=[pl.BlockSpec(memory_space=pltpu.VMEM)] + [outside] * len(held),
        out_specs=outside,
        scratch_shapes=[pltpu.SemaphoreType.DMA],
        input_output_aliases={1 + i: i for i in range(len(held))},
        compiler_params=pltpu.CompilerParams(vmem_limit_bytes=VMEM_LIMIT),
    )(
        pltpu.with_memory_space_constraint(value, pltpu.VMEM),
        *[pltpu.with_memory_space_constraint(a, pltpu.HBM) for a in held],
    )


def body(node_feats, members, incidence_mask, degrees, w_query, w_key, w_value, w_out):
    bf16, f32 = jnp.bfloat16, jnp.float32
    chips = lax.axis_size("node") // CORES
    edges = lax.axis_size("edge")
    part, width = node_feats.shape
    half = width // CORES
    owned = degrees.shape[0]
    pair = owned * CORES
    _, shard = members.shape[1:]
    rows = width // edges
    piece = rows + 8

    feats_other = swap_cores(node_feats)
    (packed,) = vmem_call(pack_kernel, [((part * CORES, half), bf16)])(
        fetch(node_feats), feats_other
    )
    blocks = [packed] + [send_edge(packed, step) for step in range(1, edges)]
    weights = (w_query, w_key, w_value, w_out)
    sizes = (chips, edges, owned, part)
    given = (members[0], incidence_mask[0], degrees[None])
    given += (swap_cores(given[0]), swap_cores(given[1])) + weights
    held = prepare(1 - SENDS_FIRST, sizes, (), *given)
    counts, degree, w_query, w_key, w_value, w_out = prepare(SENDS_FIRST, sizes, held, *given)
    early, late = [0, edges - 1] + list(range(1, edges - 2)), [edges - 2]
    (first,) = vmem_call(
        functools.partial(first_kernel, min(chips, 4) * pair, early), [((shard, half), f32)]
    )(counts, *[blocks[i] for i in early])
    partial = vmem_call(
        functools.partial(aggregate_kernel, chips, late), [((pair, half), f32)] + [((pair, half), bf16)] * (chips - 1)
    )(counts, first, *[blocks[i] for i in late])
    arrived = [send_chip(partial[step], step) for step in range(1, chips)]
    (scale,) = vmem_call(scale_kernel, [((pair, 128), f32)])(degree, swap_cores(degree))
    (hedge,) = vmem_call(hedge_kernel, [((pair, half), bf16)])(
        scale, partial[0], *arrived
    )

    (folded,) = vmem_call(fold_kernel, [((width, half), bf16)])(w_value, w_out)
    hedge_other = swap_cores(hedge)
    parts = vmem_call(project_kernel, [((pair, width), f32), ((pair, half), f32)])(
        hedge, w_key, folded
    )
    grams = vmem_call(
        functools.partial(gram_kernel, edges),
        [((piece, half), f32)] + [((piece, half), bf16)] * (edges - 1),
        [pltpu.VMEM((width, half), f32)],
    )(hedge_other, *parts, w_key, folded)
    arrived = [send_edge(grams[step], step) for step in range(1, edges)]
    (query,) = vmem_call(query_kernel, [((pair, width), bf16)])(
        hedge, hedge_other, w_query
    )
    plane, plane16 = vmem_call(
        functools.partial(add_kernel, count=edges - 1), [((piece, half), f32), ((piece, half), bf16)]
    )(grams[0], *arrived)
    arrived = [send_chip(plane16, step) for step in range(1, chips)]
    whole, strip = vmem_call(
        functools.partial(add_kernel, count=chips - 1), [((piece, half), bf16), ((rows, half), bf16)]
    )(plane, *arrived)
    pieces = [whole] + [send_edge(strip, step) for step in range(1, edges)]
    (denom,) = vmem_call(denom_kernel, [((pair, 128), f32)])(query, whole)
    halves, held = [((owned, half), bf16)] * CORES, pltpu.VMEM((pair, half), bf16)
    if rows % 128 == 0:
        (numer,) = vmem_call(
            functools.partial(numer_kernel, edges, early), [((pair, half), f32)]
        )(query, *[pieces[i] for i in early])
        mine, other = vmem_call(
            functools.partial(attend_kernel, edges, late), halves, [held]
        )(hedge, query, denom, numer, *[pieces[i] for i in late])
    else:
        mine, other = vmem_call(
            functools.partial(gather_kernel, edges), halves, [held, pltpu.VMEM((width, half), bf16)]
        )(hedge, query, denom, *pieces)
    arrived = swap_cores(other)
    return store(1, arrived, store(0, mine))


def solution(mesh):
    placed = (
        P(("node", "edge"), None),
        P("node", None, "edge"),
        P("node", None, "edge"),
        P(("edge", "node")),
        P(),
        P(),
        P(),
        P(),
    )
    return jax.shard_map(body, mesh=mesh, in_specs=placed, out_specs=P(("edge", "node"), None), check_vma=False)
```

```python
import functools

import jax
import jax.numpy as jnp
from jax import lax
from jax.experimental import pallas as pl
from jax.experimental.pallas import tpu as pltpu
from jax.sharding import PartitionSpec as P


VMEM_LIMIT = 16 * 2**20

SENDS_FIRST = 1
CORES = 2


def to_peer(index, step, count):
    if count & (count - 1) == 0:
        return index ^ step
    return (index + step) % count


def from_peer(index, step, count):
    if count & (count - 1) == 0:
        return index ^ step
    return (index + count - step) % count


def swap_cores(value):
    count = lax.axis_size("node")
    return lax.ppermute(value, "node", [(i, i ^ 1) for i in range(count)])


def send_edge(value, step):
    count = lax.axis_size("edge")
    return lax.ppermute(value, "edge", [(i, to_peer(i, step, count)) for i in range(count)])


def send_chip(value, step):
    chips = lax.axis_size("node") // CORES
    return lax.ppermute(
        value,
        "node",
        [(i, to_peer(i // CORES, step, chips) * CORES + i % CORES) for i in range(chips * CORES)],
    )


def vmem_call(kernel, outs, scratch=()):
    def call(*args):
        spec = pl.BlockSpec(memory_space=pltpu.VMEM)
        return pl.pallas_call(
            kernel,
            out_shape=[pltpu.VMEM(shape, dtype) for shape, dtype in outs],
            in_specs=[spec] * len(args),
            out_specs=[spec] * len(outs),
            scratch_shapes=list(scratch),
            compiler_params=pltpu.CompilerParams(vmem_limit_bytes=VMEM_LIMIT),
        )(*[pltpu.with_memory_space_constraint(a, pltpu.VMEM) for a in args])

    return call


def fetch_kernel(source, out, sem):
    here, _ = half_place(out.shape[1])
    move = pltpu.make_async_copy(source.at[:, here], out, sem)
    move.start()
    move.wait()


def fetch(value):
    return pl.pallas_call(
        fetch_kernel,
        out_shape=pltpu.VMEM((value.shape[0], value.shape[1] // CORES), value.dtype),
        in_specs=[pl.BlockSpec(memory_space=pltpu.HBM)],
        out_specs=pl.BlockSpec(memory_space=pltpu.VMEM),
        scratch_shapes=[pltpu.SemaphoreType.DMA],
        compiler_params=pltpu.CompilerParams(vmem_limit_bytes=VMEM_LIMIT),
        name="fetch",
    )(pltpu.with_memory_space_constraint(value, pltpu.HBM))


def feature_map(values):
    return jnp.where(values > 0, values + 1.0, jnp.exp(jnp.minimum(values, 0.0)))


def half_place(half):
    core = lax.axis_index("node") % CORES
    mine = pl.ds(pl.multiple_of(core * half, half), half)
    other = pl.ds(pl.multiple_of((1 - core) * half, half), half)
    return mine, other


def pack_kernel(own, other, out):
    part, half = own.shape
    columns, _ = half_place(half)
    mine, theirs = half_place(part)
    out[mine, :] = own[...]
    out[theirs, :] = other[:, columns]


def prepare_kernel(turn, chips, edges, owned, part, weights, *refs):
    members, valid, degrees, members_other, valid_other = refs[:5]
    sources, refs = refs[5 : 5 + weights], refs[5 + weights :]
    if len(refs) > 7 + weights:
        refs = refs[2 + weights :]
    counts, degree = refs[:2]
    copies, (members_here, valid_here, degrees_here, columns, sems) = refs[2 : 2 + weights], refs[2 + weights :]
    core = lax.axis_index("node") % CORES
    slots = members.shape[0]

    @pl.when(core == turn)
    def work():
        moves = [
            pltpu.make_async_copy(source, target, sems.at[i])
            for i, (source, target) in enumerate(
                zip(
                    (members, valid, degrees) + tuple(sources),
                    (members_here, valid_here, degrees_here) + tuple(copies),
                )
            )
        ]
        for move in moves:
            move.start()
        for move in moves[:3]:
            move.wait()
        degree[...] = jnp.ones(degree.shape, degree.dtype)
        degree[:1, :owned] = degrees_here[...]
        own = jnp.where(valid_here[...] == 1, members_here[...], -1)
        other = jnp.where(valid_other[...] == 1, members_other[...], -1)
        first = jnp.where(core == 0, own, other)
        second = jnp.where(core == 0, other, own)
        columns[...] = jnp.concatenate([first, second], axis=0).T
        build_counts(chips, edges, owned, part, slots, columns, counts)
        for move in moves[3:]:
            move.wait()


def build_counts(chips, edges, owned, part, slots, columns, counts):
    chip = lax.axis_index("node") // CORES
    edge = lax.axis_index("edge")
    lanes = lax.broadcasted_iota(jnp.int32, (owned, part), 1)

    def chunk(step, turn):
        source = (to_peer(chip, step, chips) * CORES + turn) * owned
        rows = columns[pl.ds(pl.multiple_of(source, 8), owned), :]
        target = (step * CORES + turn) * owned
        if not isinstance(target, int):
            target = pl.multiple_of(target, 8)
        for side in range(CORES):
            wanted = [rows[:, side * slots + s : side * slots + s + 1] for s in range(slots)]
            for block in range(edges):
                nodes = lanes + from_peer(edge, block, edges) * part
                total = jnp.zeros((owned, part), jnp.float32)
                for column in wanted:
                    total = total + jnp.where(column == nodes, 1.0, 0.0)
                place = (block * CORES + side) * part
                counts[pl.ds(target, owned), place : place + part] = total.astype(jnp.bfloat16)

    if chips <= 4:
        for step in range(chips):
            for turn in range(CORES):
                chunk(step, turn)
    else:
        lax.fori_loop(0, chips * CORES, lambda i, _: chunk(i // CORES, i % CORES), None)


def prepare(turn, sizes, held, members, valid, degrees, members_other, valid_other, *weights):
    chips, edges, owned, part = sizes
    slots, shard = members.shape
    shapes = [((shard, CORES * edges * part), jnp.bfloat16), ((8, 128), jnp.int32)]
    shapes += [(w.shape, w.dtype) for w in weights]
    outside, spec = pl.BlockSpec(memory_space=pltpu.HBM), pl.BlockSpec(memory_space=pltpu.VMEM)
    given = [pltpu.with_memory_space_constraint(a, pltpu.HBM) for a in (members, valid, degrees)]
    given += [pltpu.with_memory_space_constraint(a, pltpu.VMEM) for a in (members_other, valid_other)]
    given += [pltpu.with_memory_space_constraint(a, pltpu.HBM) for a in weights]
    specs = [outside] * 3 + [spec] * 2 + [outside] * len(weights)
    aliases = {len(given) + i: i for i in range(len(held))}
    given += [pltpu.with_memory_space_constraint(a, pltpu.VMEM) for a in held]
    specs += [spec] * len(held)
    return pl.pallas_call(
        functools.partial(prepare_kernel, turn, chips, edges, owned, part, len(weights)),
        out_shape=[pltpu.VMEM(shape, kind) for shape, kind in shapes],
        in_specs=specs,
        out_specs=[spec] * len(shapes),
        scratch_shapes=[
            pltpu.VMEM(members.shape, members.dtype),
            pltpu.VMEM(valid.shape, valid.dtype),
            pltpu.VMEM(degrees.shape, degrees.dtype),
            pltpu.VMEM((shard, CORES * slots), jnp.int32),
            pltpu.SemaphoreType.DMA((3 + len(weights),)),
        ],
        input_output_aliases=aliases,
        compiler_params=pltpu.CompilerParams(vmem_limit_bytes=VMEM_LIMIT),
    )(*given)


def scale_kernel(degree, degree_other, scale):
    core = lax.axis_index("node") % CORES
    owned = scale.shape[0] // CORES
    for here, ref in ((core, degree), (1 - core, degree_other)):
        line = jnp.maximum(ref[:1, :], 1).astype(jnp.float32)
        column = jnp.broadcast_to(line, (128, 128)).T
        scale[pl.ds(pl.multiple_of(here * owned, 8), owned), :] = column[:owned, :]


def blocks_sum(counts, place, blocks, used):
    nodes = blocks[0].shape[0]
    total = None
    for ref, block in zip(blocks, used):
        term = jnp.dot(
            counts[place, block * nodes : (block + 1) * nodes], ref[...], preferred_element_type=jnp.float32
        )
        total = term if total is None else total + term
    return total


def first_kernel(group, used, counts, *refs):
    blocks, out = refs[:-1], refs[-1]
    for start in range(0, out.shape[0], group):
        place = pl.ds(start, group)
        out[place, :] = blocks_sum(counts, place, blocks, used)


def aggregate_kernel(chips, used, counts, first, *refs):
    blocks, outs = refs[: len(used)], refs[len(used) :]
    rows = outs[0].shape[0]
    group = min(chips, 4)
    for start in range(0, chips, group):
        place = pl.ds(start * rows, group * rows)
        total = first[place, :] + blocks_sum(counts, place, blocks, used)
        for step in range(group):
            out = outs[start + step]
            out[...] = total[step * rows : (step + 1) * rows].astype(out.dtype)


def hedge_kernel(scale, own, *refs):
    received, out = refs[:-1], refs[-1]
    total = own[...]
    for ref in received:
        total = total + ref[...].astype(jnp.float32)
    out[...] = (total / scale[:, :1]).astype(out.dtype)


def fold_kernel(w_value, w_out, folded):
    mine, _ = half_place(folded.shape[1])
    folded[...] = jnp.dot(w_value[...], w_out[:, mine], preferred_element_type=jnp.float32).astype(
        folded.dtype
    )


def project_kernel(hedge, w_key, folded, key_part, value_part):
    mine, _ = half_place(hedge.shape[1])
    key_part[...] = jnp.dot(hedge[...], w_key[mine, :], preferred_element_type=jnp.float32)
    value_part[...] = jnp.dot(hedge[...], folded[mine, :], preferred_element_type=jnp.float32)


def gram_kernel(edges, hedge_other, key_part, value_part, w_key, folded, *refs):
    outs, gram = refs[:edges], refs[edges]
    edge = lax.axis_index("edge")
    width = w_key.shape[0]
    half = width // CORES
    rows = width // edges
    _, other = half_place(half)
    both = hedge_other[...]
    keys = key_part[...] + jnp.dot(both, w_key[other, :], preferred_element_type=jnp.float32)
    keys = feature_map(keys).astype(jnp.bfloat16)
    values = value_part[...] + jnp.dot(both, folded[other, :], preferred_element_type=jnp.float32)
    gram[...] = lax.dot_general(
        keys, values.astype(jnp.bfloat16), (((0,), (0,)), ((), ())), preferred_element_type=jnp.float32
    )
    key_sum = jnp.sum(keys.astype(jnp.float32), axis=0, keepdims=True)
    tail = [key_sum[:, i * half : (i + 1) * half] for i in range(CORES)]
    tail = jnp.concatenate(tail + [jnp.zeros((8 - CORES, half), jnp.float32)], axis=0)
    for step in range(edges):
        first = pl.multiple_of(to_peer(edge, step, edges) * rows, rows)
        outs[step][:rows, :] = gram[pl.ds(first, rows), :].astype(outs[step].dtype)
        outs[step][rows:, :] = tail.astype(outs[step].dtype)


def query_kernel(hedge, hedge_other, w_query, out):
    mine, other = half_place(hedge.shape[1])
    total = jnp.dot(hedge[...], w_query[mine, :], preferred_element_type=jnp.float32)
    total = total + jnp.dot(hedge_other[...], w_query[other, :], preferred_element_type=jnp.float32)
    out[...] = feature_map(total).astype(out.dtype)


def add_kernel(own, *refs, count):
    received, outs = refs[:count], refs[count:]
    total = own[...]
    for ref in received:
        total = total + ref[...].astype(jnp.float32)
    for out in outs:
        out[...] = total[: out.shape[0]].astype(out.dtype)


def numer_sum(edges, query, pieces, used):
    edge = lax.axis_index("edge")
    rows = query.shape[1] // edges
    total = None
    for ref, step in zip(pieces, used):
        place = pl.ds(pl.multiple_of(from_peer(edge, step, edges) * rows, 128), rows)
        term = jnp.dot(query[:, place], ref[:rows, :], preferred_element_type=jnp.float32)
        total = term if total is None else total + term
    return total


def denom_kernel(query, whole, out):
    half = whole.shape[1]
    tail = whole[whole.shape[0] - 8 :, :].astype(jnp.float32)
    denom = None
    for side in range(CORES):
        part = query[:, side * half : (side + 1) * half].astype(jnp.float32) * tail[side : side + 1, :]
        part = jnp.sum(part, axis=1, keepdims=True)
        denom = part if denom is None else denom + part
    out[...] = jnp.broadcast_to(denom, out.shape)


def numer_kernel(edges, used, query, *refs):
    refs[-1][...] = numer_sum(edges, query, refs[:-1], used)


def attend_kernel(edges, used, hedge, query, denom, numer, *refs):
    pieces, (mine, other, mixed) = refs[: len(used)], refs[len(used) :]
    total = numer[...] + numer_sum(edges, query, pieces, used)
    mix_rows(hedge, total / denom[:, :1], mixed, mine, other)


def gather_kernel(edges, hedge, query, denom, *refs):
    pieces, (mine, other, mixed, gram) = refs[:edges], refs[edges:]
    edge = lax.axis_index("edge")
    rows = query.shape[1] // edges
    for step in range(edges):
        first = pl.multiple_of(from_peer(edge, step, edges) * rows, rows)
        gram[pl.ds(first, rows), :] = pieces[step][:rows, :]
    numer = jnp.dot(query[...], gram[...], preferred_element_type=jnp.float32)
    mix_rows(hedge, numer / denom[:, :1], mixed, mine, other)


def mix_rows(hedge, attended, mixed, mine, other):
    mixed[...] = (hedge[...].astype(jnp.float32) + attended).astype(mixed.dtype)
    here, there = half_place(mine.shape[0])
    mine[...] = mixed[here, :]
    other[...] = mixed[there, :]


def store_kernel(side, value, *refs):
    out, sem = refs[-2:]
    move = pltpu.make_async_copy(value, out.at[:, half_place(value.shape[1])[side]], sem)
    move.start()
    move.wait()


def store(side, value, *held):
    outside = pl.BlockSpec(memory_space=pltpu.HBM)
    return pl.pallas_call(
        functools.partial(store_kernel, side),
        out_shape=pltpu.HBM((value.shape[0], CORES * value.shape[1]), value.dtype),
        in_specs=[pl.BlockSpec(memory_space=pltpu.VMEM)] + [outside] * len(held),
        out_specs=outside,
        scratch_shapes=[pltpu.SemaphoreType.DMA],
        input_output_aliases={1 + i: i for i in range(len(held))},
        compiler_params=pltpu.CompilerParams(vmem_limit_bytes=VMEM_LIMIT),
    )(
        pltpu.with_memory_space_constraint(value, pltpu.VMEM),
        *[pltpu.with_memory_space_constraint(a, pltpu.HBM) for a in held],
    )


def body(node_feats, members, incidence_mask, degrees, w_query, w_key, w_value, w_out):
    bf16, f32 = jnp.bfloat16, jnp.float32
    chips = lax.axis_size("node") // CORES
    edges = lax.axis_size("edge")
    part, width = node_feats.shape
    half = width // CORES
    owned = degrees.shape[0]
    pair = owned * CORES
    _, shard = members.shape[1:]
    rows = width // edges
    piece = rows + 8

    feats_other = swap_cores(node_feats)
    (packed,) = vmem_call(pack_kernel, [((part * CORES, half), bf16)])(
        fetch(node_feats), feats_other
    )
    blocks = [packed] + [send_edge(packed, step) for step in range(1, edges)]
    weights = (w_query, w_key, w_value, w_out)
    sizes = (chips, edges, owned, part)
    given = (members[0], incidence_mask[0], degrees[None])
    given += (swap_cores(given[0]), swap_cores(given[1])) + weights
    held = prepare(1 - SENDS_FIRST, sizes, (), *given)
    counts, degree, w_query, w_key, w_value, w_out = prepare(SENDS_FIRST, sizes, held, *given)
    early, late = [0, edges - 1] + list(range(1, edges - 2)), [edges - 2]
    (first,) = vmem_call(
        functools.partial(first_kernel, min(chips, 4) * pair, early), [((shard, half), f32)]
    )(counts, *[blocks[i] for i in early])
    partial = vmem_call(
        functools.partial(aggregate_kernel, chips, late), [((pair, half), f32)] + [((pair, half), bf16)] * (chips - 1)
    )(counts, first, *[blocks[i] for i in late])
    arrived = [send_chip(partial[step], step) for step in range(1, chips)]
    (scale,) = vmem_call(scale_kernel, [((pair, 128), f32)])(degree, swap_cores(degree))
    (hedge,) = vmem_call(hedge_kernel, [((pair, half), bf16)])(
        scale, partial[0], *arrived
    )

    (folded,) = vmem_call(fold_kernel, [((width, half), bf16)])(w_value, w_out)
    hedge_other = swap_cores(hedge)
    parts = vmem_call(project_kernel, [((pair, width), f32), ((pair, half), f32)])(
        hedge, w_key, folded
    )
    grams = vmem_call(
        functools.partial(gram_kernel, edges),
        [((piece, half), f32)] + [((piece, half), bf16)] * (edges - 1),
        [pltpu.VMEM((width, half), f32)],
    )(hedge_other, *parts, w_key, folded)
    arrived = [send_edge(grams[step], step) for step in range(1, edges)]
    (query,) = vmem_call(query_kernel, [((pair, width), bf16)])(
        hedge, hedge_other, w_query
    )
    plane, plane16 = vmem_call(
        functools.partial(add_kernel, count=edges - 1), [((piece, half), f32), ((piece, half), bf16)]
    )(grams[0], *arrived)
    arrived = [send_chip(plane16, step) for step in range(1, chips)]
    whole, strip = vmem_call(
        functools.partial(add_kernel, count=chips - 1), [((piece, half), bf16), ((rows, half), bf16)]
    )(plane, *arrived)
    pieces = [whole] + [send_edge(strip, step) for step in range(1, edges)]
    (denom,) = vmem_call(denom_kernel, [((pair, 128), f32)])(query, whole)
    halves, held = [((owned, half), bf16)] * CORES, pltpu.VMEM((pair, half), bf16)
    if rows % 128 == 0:
        (numer,) = vmem_call(
            functools.partial(numer_kernel, edges, early), [((pair, half), f32)]
        )(query, *[pieces[i] for i in early])
        mine, other = vmem_call(
            functools.partial(attend_kernel, edges, late), halves, [held]
        )(hedge, query, denom, numer, *[pieces[i] for i in late])
    else:
        mine, other = vmem_call(
            functools.partial(gather_kernel, edges), halves, [held, pltpu.VMEM((width, half), bf16)]
        )(hedge, query, denom, *pieces)
    arrived = swap_cores(other)
    return store(1, arrived, store(0, mine))


def solution(mesh):
    placed = (
        P(("node", "edge"), None),
        P("node", None, "edge"),
        P("node", None, "edge"),
        P(("edge", "node")),
        P(),
        P(),
        P(),
        P(),
    )
    return jax.shard_map(body, mesh=mesh, in_specs=placed, out_specs=P(("edge", "node"), None), check_vma=False)
```

```python
import functools

import jax
import jax.numpy as jnp
from jax import lax
from jax.experimental import pallas as pl
from jax.experimental.pallas import tpu as pltpu
from jax.sharding import PartitionSpec as P


VMEM_LIMIT = 16 * 2**20

SENDS_FIRST = 1
CORES = 2


def to_peer(index, step, count):
    if count & (count - 1) == 0:
        return index ^ step
    return (index + step) % count


def from_peer(index, step, count):
    if count & (count - 1) == 0:
        return index ^ step
    return (index + count - step) % count


def swap_cores(value):
    count = lax.axis_size("node")
    return lax.ppermute(value, "node", [(i, i ^ 1) for i in range(count)])


def send_edge(value, step):
    count = lax.axis_size("edge")
    return lax.ppermute(value, "edge", [(i, to_peer(i, step, count)) for i in range(count)])


def send_chip(value, step):
    chips = lax.axis_size("node") // CORES
    return lax.ppermute(
        value,
        "node",
        [(i, to_peer(i // CORES, step, chips) * CORES + i % CORES) for i in range(chips * CORES)],
    )


def vmem_call(kernel, outs, scratch=()):
    def call(*args):
        spec = pl.BlockSpec(memory_space=pltpu.VMEM)
        return pl.pallas_call(
            kernel,
            out_shape=[pltpu.VMEM(shape, dtype) for shape, dtype in outs],
            in_specs=[spec] * len(args),
            out_specs=[spec] * len(outs),
            scratch_shapes=list(scratch),
            compiler_params=pltpu.CompilerParams(vmem_limit_bytes=VMEM_LIMIT),
        )(*[pltpu.with_memory_space_constraint(a, pltpu.VMEM) for a in args])

    return call


def fetch_kernel(source, out, sem):
    here, _ = half_place(out.shape[1])
    move = pltpu.make_async_copy(source.at[:, here], out, sem)
    move.start()
    move.wait()


def fetch(value):
    return pl.pallas_call(
        fetch_kernel,
        out_shape=pltpu.VMEM((value.shape[0], value.shape[1] // CORES), value.dtype),
        in_specs=[pl.BlockSpec(memory_space=pltpu.HBM)],
        out_specs=pl.BlockSpec(memory_space=pltpu.VMEM),
        scratch_shapes=[pltpu.SemaphoreType.DMA],
        compiler_params=pltpu.CompilerParams(vmem_limit_bytes=VMEM_LIMIT),
        name="fetch",
    )(pltpu.with_memory_space_constraint(value, pltpu.HBM))


def feature_map(values):
    return jnp.where(values > 0, values + 1.0, jnp.exp(jnp.minimum(values, 0.0)))


def half_place(half):
    core = lax.axis_index("node") % CORES
    mine = pl.ds(pl.multiple_of(core * half, half), half)
    other = pl.ds(pl.multiple_of((1 - core) * half, half), half)
    return mine, other


def pack_kernel(own, other, out):
    part, half = own.shape
    columns, _ = half_place(half)
    mine, theirs = half_place(part)
    out[mine, :] = own[...]
    out[theirs, :] = other[:, columns]


def prepare_kernel(turn, chips, edges, owned, part, weights, *refs):
    members, valid, degrees, members_other, valid_other = refs[:5]
    sources, refs = refs[5 : 5 + weights], refs[5 + weights :]
    if len(refs) > 7 + weights:
        refs = refs[2 + weights :]
    counts, degree = refs[:2]
    copies, (members_here, valid_here, degrees_here, columns, sems) = refs[2 : 2 + weights], refs[2 + weights :]
    core = lax.axis_index("node") % CORES
    slots = members.shape[0]

    @pl.when(core == turn)
    def work():
        moves = [
            pltpu.make_async_copy(source, target, sems.at[i])
            for i, (source, target) in enumerate(
                zip(
                    (members, valid, degrees) + tuple(sources),
                    (members_here, valid_here, degrees_here) + tuple(copies),
                )
            )
        ]
        for move in moves:
            move.start()
        for move in moves[:3]:
            move.wait()
        degree[...] = jnp.ones(degree.shape, degree.dtype)
        degree[:1, :owned] = degrees_here[...]
        own = jnp.where(valid_here[...] == 1, members_here[...], -1)
        other = jnp.where(valid_other[...] == 1, members_other[...], -1)
        first = jnp.where(core == 0, own, other)
        second = jnp.where(core == 0, other, own)
        columns[...] = jnp.concatenate([first, second], axis=0).T
        build_counts(chips, edges, owned, part, slots, columns, counts)
        for move in moves[3:]:
            move.wait()


def build_counts(chips, edges, owned, part, slots, columns, counts):
    chip = lax.axis_index("node") // CORES
    edge = lax.axis_index("edge")
    lanes = lax.broadcasted_iota(jnp.int32, (owned, part), 1)

    def chunk(step, turn):
        source = (to_peer(chip, step, chips) * CORES + turn) * owned
        rows = columns[pl.ds(pl.multiple_of(source, 8), owned), :]
        target = (step * CORES + turn) * owned
        if not isinstance(target, int):
            target = pl.multiple_of(target, 8)
        for side in range(CORES):
            wanted = [rows[:, side * slots + s : side * slots + s + 1] for s in range(slots)]
            for block in range(edges):
                nodes = lanes + from_peer(edge, block, edges) * part
                total = jnp.zeros((owned, part), jnp.float32)
                for column in wanted:
                    total = total + jnp.where(column == nodes, 1.0, 0.0)
                place = (block * CORES + side) * part
                counts[pl.ds(target, owned), place : place + part] = total.astype(jnp.bfloat16)

    if chips <= 4:
        for step in range(chips):
            for turn in range(CORES):
                chunk(step, turn)
    else:
        lax.fori_loop(0, chips * CORES, lambda i, _: chunk(i // CORES, i % CORES), None)


def prepare(turn, sizes, held, members, valid, degrees, members_other, valid_other, *weights):
    chips, edges, owned, part = sizes
    slots, shard = members.shape
    shapes = [((shard, CORES * edges * part), jnp.bfloat16), ((8, 128), jnp.int32)]
    shapes += [(w.shape, w.dtype) for w in weights]
    outside, spec = pl.BlockSpec(memory_space=pltpu.HBM), pl.BlockSpec(memory_space=pltpu.VMEM)
    given = [pltpu.with_memory_space_constraint(a, pltpu.HBM) for a in (members, valid, degrees)]
    given += [pltpu.with_memory_space_constraint(a, pltpu.VMEM) for a in (members_other, valid_other)]
    given += [pltpu.with_memory_space_constraint(a, pltpu.HBM) for a in weights]
    specs = [outside] * 3 + [spec] * 2 + [outside] * len(weights)
    aliases = {len(given) + i: i for i in range(len(held))}
    given += [pltpu.with_memory_space_constraint(a, pltpu.VMEM) for a in held]
    specs += [spec] * len(held)
    return pl.pallas_call(
        functools.partial(prepare_kernel, turn, chips, edges, owned, part, len(weights)),
        out_shape=[pltpu.VMEM(shape, kind) for shape, kind in shapes],
        in_specs=specs,
        out_specs=[spec] * len(shapes),
        scratch_shapes=[
            pltpu.VMEM(members.shape, members.dtype),
            pltpu.VMEM(valid.shape, valid.dtype),
            pltpu.VMEM(degrees.shape, degrees.dtype),
            pltpu.VMEM((shard, CORES * slots), jnp.int32),
            pltpu.SemaphoreType.DMA((3 + len(weights),)),
        ],
        input_output_aliases=aliases,
        compiler_params=pltpu.CompilerParams(vmem_limit_bytes=VMEM_LIMIT),
    )(*given)


def scale_kernel(degree, degree_other, scale):
    core = lax.axis_index("node") % CORES
    owned = scale.shape[0] // CORES
    for here, ref in ((core, degree), (1 - core, degree_other)):
        line = jnp.maximum(ref[:1, :], 1).astype(jnp.float32)
        column = jnp.broadcast_to(line, (128, 128)).T
        scale[pl.ds(pl.multiple_of(here * owned, 8), owned), :] = column[:owned, :]


def blocks_sum(counts, place, blocks, used):
    nodes = blocks[0].shape[0]
    total = None
    for ref, block in zip(blocks, used):
        term = jnp.dot(
            counts[place, block * nodes : (block + 1) * nodes], ref[...], preferred_element_type=jnp.float32
        )
        total = term if total is None else total + term
    return total


def first_kernel(group, used, counts, *refs):
    blocks, out = refs[:-1], refs[-1]
    for start in range(0, out.shape[0], group):
        place = pl.ds(start, group)
        out[place, :] = blocks_sum(counts, place, blocks, used)


def aggregate_kernel(chips, used, counts, first, *refs):
    blocks, outs = refs[: len(used)], refs[len(used) :]
    rows = outs[0].shape[0]
    group = min(chips, 4)
    for start in range(0, chips, group):
        place = pl.ds(start * rows, group * rows)
        total = first[place, :] + blocks_sum(counts, place, blocks, used)
        for step in range(group):
            out = outs[start + step]
            out[...] = total[step * rows : (step + 1) * rows].astype(out.dtype)


def hedge_kernel(scale, own, *refs):
    received, out = refs[:-1], refs[-1]
    total = own[...]
    for ref in received:
        total = total + ref[...].astype(jnp.float32)
    out[...] = (total / scale[:, :1]).astype(out.dtype)


def project_kernel(hedge, w_key, w_value, key_part, value_part):
    mine, _ = half_place(hedge.shape[1])
    key_part[...] = jnp.dot(hedge[...], w_key[mine, :], preferred_element_type=jnp.float32)
    value_part[...] = jnp.dot(hedge[...], w_value[mine, mine], preferred_element_type=jnp.float32)


def gram_kernel(edges, hedge_other, key_part, value_part, w_key, w_value, *refs):
    outs, gram = refs[:edges], refs[edges]
    edge = lax.axis_index("edge")
    width = w_key.shape[0]
    half = width // CORES
    rows = width // edges
    mine, other = half_place(half)
    both = hedge_other[...]
    keys = key_part[...] + jnp.dot(both, w_key[other, :], preferred_element_type=jnp.float32)
    keys = feature_map(keys).astype(jnp.bfloat16)
    values = value_part[...] + jnp.dot(both, w_value[other, mine], preferred_element_type=jnp.float32)
    gram[...] = lax.dot_general(
        keys, values.astype(jnp.bfloat16), (((0,), (0,)), ((), ())), preferred_element_type=jnp.float32
    )
    key_sum = jnp.sum(keys.astype(jnp.float32), axis=0, keepdims=True)
    tail = [key_sum[:, i * half : (i + 1) * half] for i in range(CORES)]
    tail = jnp.concatenate(tail + [jnp.zeros((8 - CORES, half), jnp.float32)], axis=0)
    for step in range(edges):
        first = pl.multiple_of(to_peer(edge, step, edges) * rows, rows)
        outs[step][:rows, :] = gram[pl.ds(first, rows), :].astype(outs[step].dtype)
        outs[step][rows:, :] = tail.astype(outs[step].dtype)


def query_kernel(hedge, hedge_other, w_query, out, full):
    mine, other = half_place(hedge.shape[1])
    full[:, mine] = hedge[...]
    full[:, other] = hedge_other[...]
    out[...] = feature_map(
        jnp.dot(full[...], w_query[...], preferred_element_type=jnp.float32)
    ).astype(out.dtype)


def add_kernel(own, *refs, count):
    received, outs = refs[:count], refs[count:]
    total = own[...]
    for ref in received:
        total = total + ref[...].astype(jnp.float32)
    for out in outs:
        out[...] = total[: out.shape[0]].astype(out.dtype)


def numer_sum(edges, query, pieces, used):
    edge = lax.axis_index("edge")
    rows = query.shape[1] // edges
    total = None
    for ref, step in zip(pieces, used):
        place = pl.ds(pl.multiple_of(from_peer(edge, step, edges) * rows, 128), rows)
        term = jnp.dot(query[:, place], ref[:rows, :], preferred_element_type=jnp.float32)
        total = term if total is None else total + term
    return total


def denom_kernel(query, whole, out):
    half = whole.shape[1]
    tail = whole[whole.shape[0] - 8 :, :].astype(jnp.float32)
    denom = None
    for side in range(CORES):
        part = query[:, side * half : (side + 1) * half].astype(jnp.float32) * tail[side : side + 1, :]
        part = jnp.sum(part, axis=1, keepdims=True)
        denom = part if denom is None else denom + part
    out[...] = jnp.broadcast_to(denom, out.shape)


def numer_kernel(edges, used, query, *refs):
    refs[-1][...] = numer_sum(edges, query, refs[:-1], used)


def attend_kernel(edges, used, query, denom, numer, *refs):
    pieces, (mine, other, attended) = refs[: len(used)], refs[len(used) :]
    total = numer[...] + numer_sum(edges, query, pieces, used)
    attended[...] = (total / denom[:, :1]).astype(attended.dtype)
    split_rows(attended, mine, other)


def gather_kernel(edges, query, denom, *refs):
    pieces, (mine, other, attended, gram) = refs[:edges], refs[edges:]
    edge = lax.axis_index("edge")
    rows = query.shape[1] // edges
    for step in range(edges):
        first = pl.multiple_of(from_peer(edge, step, edges) * rows, rows)
        gram[pl.ds(first, rows), :] = pieces[step][:rows, :]
    numer = jnp.dot(query[...], gram[...], preferred_element_type=jnp.float32)
    attended[...] = (numer / denom[:, :1]).astype(attended.dtype)
    split_rows(attended, mine, other)


def split_rows(attended, mine, other):
    here, there = half_place(mine.shape[0])
    mine[...] = attended[here, :]
    other[...] = attended[there, :]


def base_kernel(full, mine, w_out, out):
    here, _ = half_place(mine.shape[0])
    rows, _ = half_place(mine.shape[1])
    out[...] = full[here, :].astype(jnp.float32) + jnp.dot(
        mine[...], w_out[rows, :], preferred_element_type=jnp.float32
    )


def output_kernel(base, other, w_out, out, result, sems):
    _, rows = half_place(other.shape[1])
    half = other.shape[1]
    moves = []
    for side in range(CORES):
        place = pl.ds(side * half, half)
        mixed = base[:, place] + jnp.dot(
            other[...], w_out[rows, place], preferred_element_type=jnp.float32
        )
        result[:, place] = mixed.astype(result.dtype)
        moves.append(pltpu.make_async_copy(result.at[:, place], out.at[:, place], sems.at[side]))
        moves[-1].start()
    for move in moves:
        move.wait()


def write_output(base, other, w_out):
    args = (base, other, w_out)
    spec = pl.BlockSpec(memory_space=pltpu.VMEM)
    return pl.pallas_call(
        output_kernel,
        out_shape=pltpu.HBM(base.shape, other.dtype),
        in_specs=[spec] * len(args),
        out_specs=pl.BlockSpec(memory_space=pltpu.HBM),
        scratch_shapes=[
            pltpu.VMEM(base.shape, other.dtype),
            pltpu.SemaphoreType.DMA((CORES,)),
        ],
        compiler_params=pltpu.CompilerParams(vmem_limit_bytes=VMEM_LIMIT),
        name="output",
    )(*[pltpu.with_memory_space_constraint(a, pltpu.VMEM) for a in args])


def body(node_feats, members, incidence_mask, degrees, w_query, w_key, w_value, w_out):
    bf16, f32 = jnp.bfloat16, jnp.float32
    chips = lax.axis_size("node") // CORES
    edges = lax.axis_size("edge")
    part, width = node_feats.shape
    half = width // CORES
    owned = degrees.shape[0]
    pair = owned * CORES
    _, shard = members.shape[1:]
    rows = width // edges
    piece = rows + 8

    feats_other = swap_cores(node_feats)
    (packed,) = vmem_call(pack_kernel, [((part * CORES, half), bf16)])(
        fetch(node_feats), feats_other
    )
    blocks = [packed] + [send_edge(packed, step) for step in range(1, edges)]
    weights = (w_query, w_key, w_value, w_out)
    sizes = (chips, edges, owned, part)
    given = (members[0], incidence_mask[0], degrees[None])
    given += (swap_cores(given[0]), swap_cores(given[1])) + weights
    held = prepare(1 - SENDS_FIRST, sizes, (), *given)
    counts, degree, w_query, w_key, w_value, w_out = prepare(SENDS_FIRST, sizes, held, *given)
    early, late = [0, edges - 1] + list(range(1, edges - 2)), [edges - 2]
    (first,) = vmem_call(
        functools.partial(first_kernel, min(chips, 4) * pair, early), [((shard, half), f32)]
    )(counts, *[blocks[i] for i in early])
    partial = vmem_call(
        functools.partial(aggregate_kernel, chips, late), [((pair, half), f32)] + [((pair, half), bf16)] * (chips - 1)
    )(counts, first, *[blocks[i] for i in late])
    arrived = [send_chip(partial[step], step) for step in range(1, chips)]
    (scale,) = vmem_call(scale_kernel, [((pair, 128), f32)])(degree, swap_cores(degree))
    (hedge,) = vmem_call(hedge_kernel, [((pair, half), bf16)])(
        scale, partial[0], *arrived
    )

    hedge_other = swap_cores(hedge)
    parts = vmem_call(project_kernel, [((pair, width), f32), ((pair, half), f32)])(hedge, w_key, w_value)
    grams = vmem_call(
        functools.partial(gram_kernel, edges),
        [((piece, half), f32)] + [((piece, half), bf16)] * (edges - 1),
        [pltpu.VMEM((width, half), f32)],
    )(hedge_other, *parts, w_key, w_value)
    arrived = [send_edge(grams[step], step) for step in range(1, edges)]
    query, full = vmem_call(query_kernel, [((pair, width), bf16)] * 2)(
        hedge, hedge_other, w_query
    )
    plane, plane16 = vmem_call(
        functools.partial(add_kernel, count=edges - 1), [((piece, half), f32), ((piece, half), bf16)]
    )(grams[0], *arrived)
    arrived = [send_chip(plane16, step) for step in range(1, chips)]
    whole, strip = vmem_call(
        functools.partial(add_kernel, count=chips - 1), [((piece, half), bf16), ((rows, half), bf16)]
    )(plane, *arrived)
    pieces = [whole] + [send_edge(strip, step) for step in range(1, edges)]
    (denom,) = vmem_call(denom_kernel, [((pair, 128), f32)])(query, whole)
    halves, held = [((owned, half), bf16)] * CORES, pltpu.VMEM((pair, half), bf16)
    if rows % 128 == 0:
        (numer,) = vmem_call(
            functools.partial(numer_kernel, edges, early), [((pair, half), f32)]
        )(query, *[pieces[i] for i in early])
        mine, other = vmem_call(
            functools.partial(attend_kernel, edges, late), halves, [held]
        )(query, denom, numer, *[pieces[i] for i in late])
    else:
        mine, other = vmem_call(
            functools.partial(gather_kernel, edges), halves, [held, pltpu.VMEM((width, half), bf16)]
        )(query, denom, *pieces)
    arrived = swap_cores(other)
    (base,) = vmem_call(base_kernel, [((owned, width), f32)])(full, mine, w_out)
    return write_output(base, arrived, w_out)


def solution(mesh):
    placed = (
        P(("node", "edge"), None),
        P("node", None, "edge"),
        P("node", None, "edge"),
        P(("edge", "node")),
        P(),
        P(),
        P(),
        P(),
    )
    return jax.shard_map(body, mesh=mesh, in_specs=placed, out_specs=P(("edge", "node"), None), check_vma=False)
```
